32 devices in a mesh: dp: 8 (over z, y), chan: 4 (over x, core).
Axes of the slice: x: 2, y: 2, z: 4, core: 2. Of those that a mesh axis runs over, the one named last changes fastest.
Arguments:
- images: bfloat16 [256, 10, 14, 1536], P('dp', None, None, 'chan'), may hold values from -6 to 6
- aspect: int32 [256], P('dp'), may hold values from 0 to 1
- reduce_weight: bfloat16 [1536, 768], P('chan'), may hold values from -400 to 400
- reduce_gain: float32 [768], replicated, may hold values from 0.1 to 1.9
- reduce_bias: float32 [768], replicated, may hold values from -3 to 3
- first_weight: bfloat16 [3, 3, 128, 768], replicated, may hold values from -6 to 6
- first_gain: float32 [768], replicated, may hold values from 0.1 to 1.9
- first_bias: float32 [768], replicated, may hold values from -3 to 3
- second_weight: bfloat16 [3, 3, 128, 768], replicated, may hold values from -6 to 6
- second_gain: float32 [768], replicated, may hold values from 0.1 to 1.9
- second_bias: float32 [768], replicated, may hold values from -3 to 3
- expand_weight: bfloat16 [768, 1536], P('chan'), may hold values from -400 to 400
- expand_gain: float32 [1536], P('chan'), may hold values from 0.1 to 1.9
- expand_bias: float32 [1536], P('chan'), may hold values from -3 to 3
- excite_down: bfloat16 [1536, 768], P('chan'), may hold values from -0.3125 to 0.3125
- excite_down_bias: float32 [768], replicated, may hold values from -3 to 3
- excite_up: bfloat16 [768, 1536], P(None, 'chan'), may hold values from -0.4375 to 0.4375
- excite_up_bias: float32 [1536], P('chan'), may hold values from -3 to 3
- skip_gain: float32 [1], replicated, may hold values from 3 to 6
- out_grad: bfloat16 [256, 10, 14, 1536], P('dp', None, None, 'chan'), may hold values from -6 to 6
Outputs:
- block_out: bfloat16 [256, 10, 14, 1536], P('dp', None, None, 'chan')
- images_grad: float32 [256, 10, 14, 1536], P('dp', None, None, 'chan')
- reduce_weight_grad: float32 [1536, 768], P('chan')
- reduce_gain_grad: float32 [768], replicated
- reduce_bias_grad: float32 [768], replicated
- first_weight_grad: float32 [3, 3, 128, 768], replicated
- first_gain_grad: float32 [768], replicated
- first_bias_grad: float32 [768], replicated
- second_weight_grad: float32 [3, 3, 128, 768], replicated
- second_gain_grad: float32 [768], replicated
- second_bias_grad: float32 [768], replicated
- expand_weight_grad: float32 [768, 1536], P('chan')
- expand_gain_grad: float32 [1536], P('chan')
- expand_bias_grad: float32 [1536], P('chan')
- excite_down_grad: float32 [1536, 768], P('chan')
- excite_down_bias_grad: float32 [768], replicated
- excite_up_grad: float32 [768, 1536], P(None, 'chan')
- excite_up_bias_grad: float32 [1536], P('chan')
- skip_gain_grad: float32 [1], replicated
The draws below stay inside these ranges and needn't reach their ends.
Inputs may be any that keep to these rules, and one draw needn't show every extreme that they name: `aspect`: 0: the image is 10 rows by 14 columns as stored; 1: it is 14 rows by 10 columns, stored transposed.
All inputs are finite; a program needn't handle non-finite values.
Results may differ from the reference program's by a relative error of at most 0.025.
The reference program's roundings to bfloat16 on the way count: a program that leaves them out, or rounds other values in their place, can miss the bound.
Values may be sent and summed in bfloat16 or wider, within the bound.
A program may use at most 256 MiB of HBM per device.

```python
import math
import jax
import jax.numpy as jnp
from jax import lax

C = 1536
M = 768
G = 128
HT = 10
WD = 14
IMAGES = 256


def scaled_matrix(key, rows, columns):
    entry_key, row_key, column_key = jax.random.split(key, 3)
    entries = jax.random.truncated_normal(entry_key, -4.0, 4.0, (rows, columns), jnp.float32)
    row_scale = jnp.exp(jax.random.uniform(row_key, (rows, 1), jnp.float32) * math.log(10.0))
    column_scale = jnp.exp(jax.random.uniform(column_key, (1, columns), jnp.float32) * math.log(10.0))
    return (entries * row_scale * column_scale).astype(jnp.bfloat16)


def draw_reduce_weight(key, part):
    return scaled_matrix(jax.random.fold_in(key, 11), C, M)


def draw_expand_weight(key, part):
    return scaled_matrix(jax.random.fold_in(key, 23), M, C)


def plant(values, stream_key, low, largest):
    index_at = [jax.random.randint(jax.random.fold_in(stream_key, axis), (), 0, length) for axis, length in enumerate(values.shape)]
    main_axis = values.shape.index(max(values.shape))
    beside = index_at[:main_axis] + [(index_at[main_axis] + 1) % values.shape[main_axis]] + index_at[main_axis + 1:]
    return values.at[tuple(index_at)].set(low).at[tuple(beside)].set(largest)


def steps_of(own_key, shape, cuts, smallest, top_value):
    def one(position, parts):
        draws = jax.random.uniform(jax.random.fold_in(jax.random.fold_in(own_key, 6), position), (parts,), jnp.float32, smallest / len(cuts), top_value / len(cuts))
        return jnp.repeat(jnp.exp(draws), shape[position] // parts).reshape((-1,) + (1,) * (len(shape) - position - 1))

    loudness = one(*cuts[0])
    for cut in cuts[1:]:
        loudness = loudness * one(*cut)
    return loudness


def centred(own_key, shape, scale, bound, cuts=(), dtype=jnp.bfloat16):
    factor_of = steps_of(own_key, shape, cuts, -0.22, 0.18) if cuts else 1.0
    values = jax.random.normal(own_key, shape, jnp.float32) * scale * factor_of
    return jnp.minimum(jnp.maximum(values, -bound), bound).astype(dtype)


def setup_inputs(seed: int = 0) -> dict:
    key_of = jax.random.split(jax.random.key(seed), 21)
    images = centred(key_of[0], (IMAGES, HT, WD, C), 1.0, 6.0, ((0, 8), (3, 4)))
    aspect = plant(jax.random.randint(key_of[1], (IMAGES,), 0, 2), jax.random.fold_in(key_of[1], 1), 0, 1).astype(jnp.int32)
    reduce_weight = draw_reduce_weight(jax.random.fold_in(key_of[20], 71), 0)
    reduce_gain = jnp.clip(1.0 + 0.18 * jax.random.normal(key_of[3], (M,), jnp.float32), 0.1, 1.9)
    reduce_bias = centred(key_of[4], (M,), 0.5, 3.0, (), jnp.float32)
    first_weight = centred(key_of[5], (3, 3, G, M), 1.0, 6.0)
    first_gain = jnp.clip(1.0 + 0.18 * jax.random.normal(key_of[6], (M,), jnp.float32), 0.1, 1.9)
    first_bias = centred(key_of[7], (M,), 0.5, 3.0, (), jnp.float32)
    second_weight = centred(key_of[8], (3, 3, G, M), 1.0, 6.0)
    second_gain = jnp.clip(1.0 + 0.18 * jax.random.normal(key_of[9], (M,), jnp.float32), 0.1, 1.9)
    second_bias = centred(key_of[10], (M,), 0.5, 3.0, (), jnp.float32)
    expand_weight = draw_expand_weight(jax.random.fold_in(key_of[20], 71), 0)
    expand_gain = jnp.clip(1.0 + 0.18 * jax.random.normal(key_of[12], (C,), jnp.float32), 0.1, 1.9)
    expand_bias = centred(key_of[13], (C,), 0.5, 3.0, ((0, 4),), jnp.float32)
    excite_down = centred(key_of[14], (C, M), (C // 4) ** -0.5, 0.3125, ((0, 4),))
    excite_down_bias = centred(key_of[15], (M,), 0.5, 3.0, (), jnp.float32)
    excite_up = centred(key_of[16], (M, C), (M // 4) ** -0.5, 0.4375, ((1, 4),))
    excite_up_bias = centred(key_of[17], (C,), 0.5, 3.0, ((0, 4),), jnp.float32)
    skip_gain = jnp.clip(jax.random.uniform(key_of[18], (1,), jnp.float32, 3.0, 6.0), 3.0, 6.0)
    out_grad = centred(key_of[19], (IMAGES, HT, WD, C), 1.0, 6.0, ((0, 8), (3, 4)))
    return {"images": images, "aspect": aspect, "reduce_weight": reduce_weight, "reduce_gain": reduce_gain, "reduce_bias": reduce_bias, "first_weight": first_weight, "first_gain": first_gain, "first_bias": first_bias, "second_weight": second_weight, "second_gain": second_gain, "second_bias": second_bias, "expand_weight": expand_weight, "expand_gain": expand_gain, "expand_bias": expand_bias, "excite_down": excite_down, "excite_down_bias": excite_down_bias, "excite_up": excite_up, "excite_up_bias": excite_up_bias, "skip_gain": skip_gain, "out_grad": out_grad}


INV_BETA = 1.0 / 1.16619037896906
ALPHA_RES = 0.2
GELU_SCALE = 1.7015
STD_EPSILON = 0.0001
PRECISE = lax.Precision.HIGHEST
NUMBERS = ('NHWC', 'HWIO', 'NHWC')

@jax.custom_vjp
def low(v):
    return lax.optimization_barrier(v.astype(jnp.bfloat16)).astype(jnp.float32)

@jax.custom_vjp
def low_back(v):
    return v

def low_keep(v):
    return (low(v), None)

def low_pass(kept, grad):
    return (grad,)

def back_keep(v):
    return (v, None)

def back_low(kept, grad):
    return (low(grad),)
low.defvjp(low_keep, low_pass)
low_back.defvjp(back_keep, back_low)

def gelu_scaled(value):
    return GELU_SCALE * jax.nn.gelu(value, approximate=True)

def standardize(weight, axes):
    middle = lax.optimization_barrier(jnp.mean(weight, axis=axes, keepdims=True))
    centered = weight - middle
    spread = lax.optimization_barrier(jnp.mean(centered * centered, axis=axes, keepdims=True))
    fan_in = 1
    for dimension in axes:
        fan_in = fan_in * weight.shape[dimension]
    return centered * lax.rsqrt(spread * fan_in + STD_EPSILON)

def to_canvas(values, aspects):
    height, width = (values.shape[1], values.shape[2])
    side = max(height, width)
    plain = jnp.pad(values, ((0, 0), (0, side - height), (0, side - width), (0, 0)))
    turned = jnp.pad(jnp.transpose(values, (0, 2, 1, 3)), ((0, 0), (0, side - width), (0, side - height), (0, 0)))
    return jnp.where((aspects == 1)[:, None, None, None], turned, plain)

def from_canvas(canvas, aspects, height, width):
    plain = canvas[:, :height, :width]
    turned = jnp.transpose(canvas[:, :width, :height], (0, 2, 1, 3))
    return jnp.where((aspects == 1)[:, None, None, None], turned, plain)

def grouped(values, kernel, aspects):
    groups = kernel.shape[3] // kernel.shape[2]
    result = lax.conv_general_dilated(to_canvas(values, aspects), kernel, (1, 1), 'SAME', dimension_numbers=NUMBERS, feature_group_count=groups, precision=PRECISE)
    return from_canvas(result, aspects, values.shape[1], values.shape[2])

def forward(pixels, aspects, weights):
    reduce_weight, reduce_gain, reduce_bias, first_weight, first_gain, first_bias, second_weight, second_gain, second_bias, expand_weight, expand_gain, expand_bias, excite_down, excite_down_bias, excite_up, excite_up_bias, skip_gain = weights
    scaled = low(pixels * INV_BETA)
    kernel_reduce = low(standardize(reduce_weight, (0,)))
    pre_reduce = low_back(jnp.einsum('nhwc,cm->nhwm', scaled, kernel_reduce, precision=PRECISE))
    act_reduce = low(gelu_scaled(reduce_gain * pre_reduce + reduce_bias))
    kernel_first = low(standardize(first_weight, (0, 1, 2)))
    pre_first = low_back(grouped(act_reduce, kernel_first, aspects))
    act_first = low(gelu_scaled(first_gain * pre_first + first_bias))
    kernel_second = low(standardize(second_weight, (0, 1, 2)))
    pre_second = low_back(grouped(act_first, kernel_second, aspects))
    act_second = low_back(low(gelu_scaled(second_gain * pre_second + second_bias)))
    kernel_expand = low(standardize(expand_weight, (0,)))
    pre_expand = low_back(jnp.einsum('nhwm,mc->nhwc', act_second, kernel_expand, precision=PRECISE))
    out_expand = expand_gain * pre_expand + expand_bias
    pooled = lax.optimization_barrier(jnp.mean(out_expand, axis=(1, 2)))
    down = jnp.dot(pooled, excite_down, precision=PRECISE) + excite_down_bias
    upper = jnp.dot(jax.nn.gelu(down, approximate=True), excite_up, precision=PRECISE) + excite_up_bias
    gating = 2.0 * jax.nn.sigmoid(upper)
    return pixels + ALPHA_RES * skip_gain[0] * out_expand * gating[:, None, None, :]

def reference(images, aspect, reduce_weight, reduce_gain, reduce_bias, first_weight, first_gain, first_bias, second_weight, second_gain, second_bias, expand_weight, expand_gain, expand_bias, excite_down, excite_down_bias, excite_up, excite_up_bias, skip_gain, out_grad):
    params = tuple((p.astype(jnp.float32) for p in (reduce_weight, reduce_gain, reduce_bias, first_weight, first_gain, first_bias, second_weight, second_gain, second_bias, expand_weight, expand_gain, expand_bias, excite_down, excite_down_bias, excite_up, excite_up_bias, skip_gain)))
    block_size = math.gcd(IMAGES, 16)
    block_count = IMAGES // block_size

    def blocked(value):
        return value.reshape((block_count, block_size) + value.shape[1:])

    def advance(running, inputs_block):
        pixels, aspects, cotangent = inputs_block

        def evaluate(values, weights):
            return forward(values, aspects, weights)
        result_block, pullback = jax.vjp(evaluate, pixels.astype(jnp.float32), params)
        grad_pixels, grad_weights = pullback(cotangent.astype(jnp.float32))
        running = jax.tree.map(lambda u, v: u + v, running, grad_weights)
        return (running, (result_block.astype(jnp.bfloat16), grad_pixels))
    starting = jax.tree.map(jnp.zeros_like, params)
    running, (results, grads) = lax.scan(advance, starting, (blocked(images), blocked(aspect), blocked(out_grad)))
    shape_full = (IMAGES, HT, WD, C)
    return (results.reshape(shape_full), grads.reshape(shape_full), running[0], running[1], running[2], running[3], running[4], running[5], running[6], running[7], running[8], running[9], running[10], running[11], running[12], running[13], running[14], running[15], running[16])
```

```python
import functools
import jax
import jax.numpy as jnp
from jax import lax
from jax.experimental import pallas as pl
from jax.experimental.pallas import tpu as pltpu
from jax.sharding import PartitionSpec as P

INV_BETA = 1.0 / 1.16619037896906
ALPHA_RES = 0.2
GELU_SCALE = 1.7015
STD_EPSILON = 0.0001
ROOT = 0.7978845608028654
CUBIC = 0.044715
MESH = pl.DeviceIdType.MESH
F32 = jnp.float32
BF16 = jnp.bfloat16
LAG = 5


def gelu(v):
    return 0.5 * v * (1.0 + jnp.tanh(ROOT * v * (1.0 + CUBIC * v * v)))


def gelu_slope(v):
    square = v * v
    t = jnp.tanh(ROOT * v * (1.0 + CUBIC * square))
    return 0.5 * (1.0 + t) + 0.5 * v * (1.0 - t * t) * ROOT * (1.0 + 3.0 * CUBIC * square)


def split3(x):
    high = x.astype(BF16)
    rest = x - high.astype(F32)
    middle = rest.astype(BF16)
    low = (rest - middle.astype(F32)).astype(BF16)
    return jnp.concatenate([high, middle, low], axis=0)


def dot3(x, w, over):
    rows = x.shape[0]
    y = lax.dot_general(split3(x), w, (((1,), (over,)), ((), ())), preferred_element_type=F32)
    return y[:rows] + y[rows : 2 * rows] + y[2 * rows :]


def dot_nt(x, w):
    return lax.dot_general(x, w, (((1,), (1,)), ((), ())), preferred_element_type=F32)


def dot_tn(x, y):
    return lax.dot_general(x, y, (((0,), (0,)), ((), ())), preferred_element_type=F32)


def place():
    d, c = lax.axis_index("dp"), lax.axis_index("chan")
    xi, ci = c // 2, c % 2
    sib = (d, xi * 2 + (1 - ci))
    xn = (d, (1 - xi) * 2 + ci)
    dg = (d, (1 - xi) * 2 + (1 - ci))
    return d, c, xi, ci, sib, xn, dg


def greet(peers):
    barrier = pltpu.get_barrier_semaphore()
    for peer in peers:
        pl.semaphore_signal(barrier, inc=1, device_id=peer, device_id_type=MESH)
    pl.semaphore_wait(barrier, len(peers))


def remote(src, dst, send, recv, peer):
    return pltpu.make_async_remote_copy(
        src_ref=src, dst_ref=dst, send_sem=send, recv_sem=recv, device_id=peer, device_id_type=MESH
    )


def patches(ref, h, group, turned, width, taps):
    lanes = slice(group * taps, (group + 1) * taps)
    shifted = [[ref[h + u, v : v + width, :, lanes] for v in range(3)] for u in range(3)]
    parts = []
    for u in range(3):
        for v in range(3):
            if u == v:
                parts.append(shifted[u][v])
            else:
                parts.append(jnp.where(turned, shifted[v][u], shifted[u][v]))
    whole = jnp.concatenate(parts, axis=-1)
    return whole.reshape(whole.shape[0] * whole.shape[1], whole.shape[2])


def conv_row(ref, h, kernel_ref, turned, width, taps):
    groups = kernel_ref.shape[1] // taps
    outs = []
    for g in range(groups):
        outs.append(
            jnp.dot(
                patches(ref, h, g, turned, width, taps),
                kernel_ref[:, g * taps : (g + 1) * taps],
                preferred_element_type=F32,
            )
        )
    whole = jnp.concatenate(outs, axis=-1)
    return whole.reshape(width, -1, whole.shape[-1])


def forward_kernel(
    dims,
    img, og, rw, ew, dn, up, fw, sw, mvec, cvec, db, asp,
    o_preE, o_og, o_img, o_as2, o_kr, o_ke, o_preR, o_preF, o_preS, o_PR, o_PF, o_kt1, o_kt2,
    o_se, o_sum, o_str, o_ste, o_vb,
    imgb, ogb, kraw, ewb, dnb, upb, fraw, sraw, st, kr, ke, k1, k2, kt1, kt2,
    preR, s1, r1, PR, PF, preF, preS, as2, preE, acc, px, hx,
    loc_img, ss_img, rs_img, loc, ss, rs, ss_st, rs_st, ss1, rs1, ss2, rs2, sx, rx, outs,
):
    H, W, NI, CS, CH, MH, M, G = dims
    d, c, xi, ci, sib, xn, dg = place()
    greet((sib, xn, dg))
    mine = pl.ds(pl.multiple_of(ci * NI, NI), NI)
    theirs = pl.ds(pl.multiple_of((1 - ci) * NI, NI), NI)
    clan = pl.ds(pl.multiple_of(ci * CS, CS), CS)
    mlan = pl.ds(pl.multiple_of(xi * MH, MH), MH)
    olan = pl.ds(pl.multiple_of((1 - xi) * MH, MH), MH)

    def img_send(h):
        return remote(img.at[h, :, theirs, :], imgb.at[h, :, :, clan], ss_img.at[h], rs_img.at[h], sib)

    def img_local(h):
        return pltpu.make_async_copy(img.at[h, :, mine, :], imgb.at[h, :, :, clan], loc_img.at[h])

    locals_ = [
        pltpu.make_async_copy(rw, kraw.at[clan, :], loc.at[0]),
        pltpu.make_async_copy(ew.at[:, pl.ds(pl.multiple_of(xi * CH, CH), CH)], ewb.at[c], loc.at[1]),
        pltpu.make_async_copy(dn, dnb.at[clan, :], loc.at[2]),
        pltpu.make_async_copy(up, upb.at[:, clan], loc.at[3]),
        pltpu.make_async_copy(fw.at[:, mlan], fraw, loc.at[4]),
        pltpu.make_async_copy(sw.at[:, mlan], sraw, loc.at[5]),
        pltpu.make_async_copy(cvec, o_vb.at[:, clan], loc.at[6]),
        pltpu.make_async_copy(og.at[:, :, mine, :], ogb.at[:, :, :, clan], loc.at[7]),
    ]
    sends = [
        remote(rw, kraw.at[clan, :], ss.at[0], rs.at[0], sib),
        remote(ew.at[:, pl.ds(pl.multiple_of(xi * CH, CH), CH)], ewb.at[c], ss.at[1], rs.at[1], sib),
        remote(dn, dnb.at[clan, :], ss.at[2], rs.at[2], sib),
        remote(up, upb.at[:, clan], ss.at[3], rs.at[3], sib),
        remote(cvec, o_vb.at[:, clan], ss.at[4], rs.at[4], sib),
        remote(og.at[:, :, theirs, :], ogb.at[:, :, :, clan], ss.at[5], rs.at[5], sib),
        remote(ew.at[:, pl.ds(pl.multiple_of((1 - xi) * CH, CH), CH)], ewb.at[c], ss.at[6], rs.at[6], xn),
        remote(ew.at[:, pl.ds(pl.multiple_of((1 - xi) * CH, CH), CH)], ewb.at[c], ss.at[7], rs.at[7], dg),
    ]
    locals_[0].start()
    sends[0].start()

    def start_img(h, carry):
        img_local(h).start()
        img_send(h).start()
        return carry

    lax.fori_loop(0, H, start_img, 0)
    for k in (4, 5, 1, 6, 2, 3, 7):
        locals_[k].start()

    locals_[0].wait()
    own = kraw[clan, :].astype(F32)
    middle = jnp.mean(own, axis=0, keepdims=True)
    away = own - middle
    st[c] = jnp.concatenate(
        [middle, jnp.sum(away * away, axis=0, keepdims=True), jnp.zeros((6, M), F32)], axis=0
    )
    stats = [remote(st.at[c], st.at[c], ss_st.at[k], rs_st.at[c], peer) for k, peer in enumerate((sib, xn, dg))]
    for s in stats:
        s.start()
    for k in (6, 7, 1, 4, 2, 3, 5):
        sends[k].start()

    edge_w = jnp.zeros((W + 2, NI, MH), BF16)
    for ref in (PR, PF):
        ref[0] = edge_w
        ref[H + 1] = edge_w
        for h in range(1, H + 1):
            ref[h, 0] = edge_w[0]
            ref[h, W + 1] = edge_w[0]
    acc[...] = jnp.zeros_like(acc)

    def stat_of(q):
        return remote(st.at[q], st.at[q], ss_st.at[0], rs_st.at[q], sib)

    for k in (1, 2, 3):
        stat_of(lax.rem(c + k, 4)).wait_recv()
    count = CS
    mean = (st[0, 0:1] + st[1, 0:1] + st[2, 0:1] + st[3, 0:1]) * 0.25
    spread = jnp.zeros_like(mean)
    for q in range(4):
        gap = st[q, 0:1] - mean
        spread = spread + st[q, 1:2] + count * gap * gap
    rate = lax.rsqrt(spread + STD_EPSILON)
    o_str[...] = jnp.concatenate([mean, rate, jnp.zeros((6, M), F32)], axis=0)
    sends[0].wait_recv()

    def kr_block(j, carry):
        rows = pl.ds(pl.multiple_of(j * 128, 128), 128)
        kr[rows, :] = ((kraw[rows, :].astype(F32) - mean) * rate).astype(BF16)
        return carry

    lax.fori_loop(0, CH // 128, kr_block, 0)

    def s1_copy(h):
        return remote(s1.at[h], r1.at[h], ss1.at[h], rs1.at[h], xn)

    def reduce_row(h, carry):
        img_local(h).wait()
        img_send(h).wait_recv()
        scaled = (imgb[h].astype(F32) * INV_BETA).astype(BF16).reshape(W * NI, CH)
        s1[h] = (
            jnp.dot(scaled, kr[:, olan], preferred_element_type=F32).astype(BF16).reshape(W, NI, MH)
        )
        s1_copy(h).start()
        preR[h] = jnp.dot(scaled, kr[:, mlan], preferred_element_type=F32).reshape(W, NI, MH)
        return carry

    lax.fori_loop(0, H, reduce_row, 0)

    for k, raw, kern, trans in ((4, fraw, k1, kt1), (5, sraw, k2, kt2)):
        locals_[k].wait()
        for g in range(MH // G):
            lanes = slice(g * G, (g + 1) * G)
            w = raw[:, lanes].astype(F32)
            w = w - jnp.mean(w, axis=0, keepdims=True)
            w = w * lax.rsqrt(jnp.sum(w * w, axis=0, keepdims=True) + STD_EPSILON)
            kern[:, lanes] = w.astype(BF16)
            for tap in range(9):
                block = kern[(8 - tap) * G : (9 - tap) * G, lanes].astype(F32)
                trans[tap * G : (tap + 1) * G, lanes] = block.T.astype(BF16)

    locals_[1].wait()
    for k, peer in ((1, sib), (6, xn), (7, dg)):
        q = peer[1]
        remote(ewb.at[q], ewb.at[q], ss.at[k], rs.at[k], peer).wait_recv()
    quarter = ewb.shape[1]
    e_stat = []
    for j in range(CH // 128):
        lanes = slice(j * 128, (j + 1) * 128)
        blocks = [ewb[q, :, lanes].astype(F32) for q in range(4)]
        total = sum(jnp.sum(b, axis=0, keepdims=True) for b in blocks)
        e_mean = total / (4 * quarter)
        blocks = [b - e_mean for b in blocks]
        squares = sum(jnp.sum(b * b, axis=0, keepdims=True) for b in blocks)
        e_rate = lax.rsqrt(squares + STD_EPSILON)
        for q in range(4):
            ke[q * quarter : (q + 1) * quarter, lanes] = (blocks[q] * e_rate).astype(BF16)
        e_stat.append(jnp.concatenate([e_mean, e_rate, jnp.zeros((6, 128), F32)], axis=0))
    o_ste[xi] = jnp.concatenate(e_stat, axis=-1)
    ste_copy = remote(o_ste.at[xi], o_ste.at[xi], sx.at[2], rx.at[2], xn)
    ste_copy.start()

    turned = jnp.broadcast_to((asp[ci] > 0.5)[None], (W, NI, G))
    reduce_gain, reduce_bias = mvec[xi, 0:1], mvec[xi, 1:2]
    first_gain, first_bias = mvec[xi, 2:3], mvec[xi, 3:4]
    second_gain, second_bias = mvec[xi, 4:5], mvec[xi, 5:6]

    locals_[7].wait()
    sends[5].wait_recv()

    def s2_copy(h):
        return remote(as2.at[h, :, :, mlan], as2.at[h, :, :, mlan], ss2.at[h], rs2.at[h], xn)

    def s2_arrival(h):
        return remote(as2.at[h, :, :, olan], as2.at[h, :, :, olan], ss2.at[h], rs2.at[h], xn)

    def wave(t, carry):
        @pl.when(t < H)
        def _():
            s1_copy(t).wait_recv()
            pre = preR[t] + r1[t].astype(F32)
            preR[t] = pre
            PR[t + 1, 1 : W + 1] = (GELU_SCALE * gelu(pre * reduce_gain + reduce_bias)).astype(BF16)

        @pl.when((t >= 1) & (t <= H))
        def _():
            pre = conv_row(PR, t - 1, k1, turned, W, G)
            preF[t - 1] = pre
            PF[t, 1 : W + 1] = (GELU_SCALE * gelu(pre * first_gain + first_bias)).astype(BF16)

        @pl.when((t >= 2) & (t <= H + 1))
        def _():
            pre = conv_row(PF, t - 2, k2, turned, W, G)
            preS[t - 2] = pre
            as2[t - 2, :, :, mlan] = (GELU_SCALE * gelu(pre * second_gain + second_bias)).astype(BF16)
            s2_copy(t - 2).start()

        @pl.when(t >= LAG)
        def _():
            h = t - LAG
            s2_arrival(h).wait_recv()
            pre = jnp.dot(as2[h].reshape(W * NI, M), ke[...], preferred_element_type=F32).reshape(W, NI, CH)
            preE[h] = pre
            grad = ogb[h].astype(F32)
            acc[0] += jnp.sum(pre, axis=0)
            acc[1] += jnp.sum(grad, axis=0)
            acc[2] += jnp.sum(grad * pre, axis=0)

        return carry

    lax.fori_loop(0, H + LAG, wave, 0)

    pairs = (
        (preE, o_preE), (ogb, o_og), (imgb, o_img), (as2, o_as2), (kr, o_kr), (ke, o_ke), (preR, o_preR),
        (preF, o_preF), (preS, o_preS), (PR, o_PR), (PF, o_PF), (kt1, o_kt1), (kt2, o_kt2),
    )
    saves = [pltpu.make_async_copy(a, b, outs.at[k]) for k, (a, b) in enumerate(pairs)]
    for s in saves:
        s.start()

    for k in (2, 3, 6):
        locals_[k].wait()
    for k in (2, 3, 4):
        sends[k].wait_recv()
    gain, bias = o_vb[0:1, :], o_vb[1:2, :]
    up_bias, branch_scale = o_vb[2:3, :], o_vb[3:4, :]
    pixels = H * W
    sum_pre, sum_grad, sum_both = acc[0], acc[1], acc[2]
    pooled = gain * (sum_pre * (1.0 / pixels)) + bias
    px[xi] = dot3(pooled, dnb[...], 0)
    p_copy = remote(px.at[xi], px.at[xi], sx.at[0], rx.at[0], xn)
    p_copy.start()
    remote(px.at[1 - xi], px.at[1 - xi], sx.at[0], rx.at[0], xn).wait_recv()
    down = px[0] + px[1] + db[...]
    hidden = gelu(down)
    upper = dot3(hidden, upb[...], 0) + up_bias
    sigma = 1.0 / (1.0 + jnp.exp(-upper))
    gating = 2.0 * sigma
    grad_gating_raw = gain * sum_both + bias * sum_grad
    grad_upper = branch_scale * grad_gating_raw * 2.0 * sigma * (1.0 - sigma)
    hx[xi] = dot3(grad_upper, upb[...], 1)
    h_copy = remote(hx.at[xi], hx.at[xi], sx.at[1], rx.at[1], xn)
    h_copy.start()
    remote(hx.at[1 - xi], hx.at[1 - xi], sx.at[1], rx.at[1], xn).wait_recv()
    grad_down = (hx[0] + hx[1]) * gelu_slope(down)
    grad_pooled = dot3(grad_down, dnb[...], 1)
    scaled_gate = branch_scale * gating
    pool_part = grad_pooled * (1.0 / pixels)
    o_se[0] = scaled_gate
    o_se[1] = pool_part
    o_se[2] = pooled
    o_se[3] = grad_down
    o_se[4] = hidden
    o_se[5] = grad_upper
    gain_grad = jnp.sum(scaled_gate * sum_both + pool_part * sum_pre, axis=0, keepdims=True)
    bias_grad = jnp.sum(scaled_gate * sum_grad + grad_pooled, axis=0, keepdims=True)
    up_bias_grad = jnp.sum(grad_upper, axis=0, keepdims=True)
    skip_row = ALPHA_RES * jnp.sum(gating * grad_gating_raw, axis=0, keepdims=True)
    down_bias_grad = jnp.sum(grad_down, axis=0, keepdims=True)
    o_sum[...] = jnp.concatenate(
        [gain_grad, bias_grad, up_bias_grad, skip_row, down_bias_grad, jnp.zeros((3, CH), F32)], axis=0
    )

    remote(o_ste.at[1 - xi], o_ste.at[1 - xi], sx.at[2], rx.at[2], xn).wait_recv()
    for s in (ste_copy, p_copy, h_copy):
        s.wait_send()
    for s in sends + stats:
        s.wait_send()

    def drain(h, carry):
        img_send(h).wait_send()
        s1_copy(h).wait_send()
        s2_copy(h).wait_send()
        return carry

    lax.fori_loop(0, H, drain, 0)
    for s in saves:
        s.wait()


def backward_kernel(
    dims,
    i_preE, i_og, i_img, i_as2, i_kr, i_ke, i_preR, i_preF, i_preS, i_PR, i_PF, i_kt1, i_kt2,
    se, vb, mvec, asp,
    o_block, o_igrad, o_De, o_Dr, o_D1, o_D2, o_sum,
    preE, ogb, imgb, as2, kr, ke, preR, preF, preS, PR, PF, kt1, kt2,
    gpe, s3, r3, GS, GF, gpr, bst, igst, pbuf,
    ld, ldr, ss3, rs3, ss4, rs4, b_loc, b_ss, b_rs, g_loc, g_ss, g_rs,
):
    H, W, NI, CS, CH, MH, M, G = dims
    d, c, xi, ci, sib, xn, dg = place()
    pairs = (
        (i_kr, kr), (i_ke, ke), (i_kt1, kt1), (i_kt2, kt2), (i_PR, PR), (i_PF, PF), (i_as2, as2),
        (i_preR, preR), (i_preF, preF), (i_preS, preS),
    )
    loads = [pltpu.make_async_copy(a, b, ld.at[k]) for k, (a, b) in enumerate(pairs)]

    def row_loads(h):
        return [
            pltpu.make_async_copy(i_preE.at[h], preE.at[h], ldr.at[h, 0]),
            pltpu.make_async_copy(i_og.at[h], ogb.at[h], ldr.at[h, 1]),
            pltpu.make_async_copy(i_img.at[h], imgb.at[h], ldr.at[h, 2]),
        ]

    loads[1].start()
    for h in range(H):
        for s in row_loads(h):
            s.start()
    for k in (6, 9, 5, 3, 8, 4, 2, 7, 0):
        loads[k].start()

    greet((sib, xn))
    mine = pl.ds(pl.multiple_of(ci * NI, NI), NI)
    clan = pl.ds(pl.multiple_of(ci * CS, CS), CS)
    slan = pl.ds(pl.multiple_of((1 - ci) * CS, CS), CS)
    mlan = pl.ds(pl.multiple_of(xi * MH, MH), MH)
    olan = pl.ds(pl.multiple_of((1 - xi) * MH, MH), MH)
    edge_w = jnp.zeros((W + 2, NI, MH), BF16)
    for ref in (GS, GF):
        ref[0] = edge_w
        ref[H + 1] = edge_w
        for h in range(1, H + 1):
            ref[h, 0] = edge_w[0]
            ref[h, W + 1] = edge_w[0]
    o_sum[...] = jnp.zeros_like(o_sum)

    gain, bias = vb[0:1, :], vb[1:2, :]
    scaled_gate, pool_part = se[0], se[1]
    slots = bst.shape[0]

    def block_local(h):
        return pltpu.make_async_copy(bst.at[lax.rem(h, slots), :, :, clan], o_block.at[h, :, mine, :], b_loc.at[h])

    def block_send(h):
        return remote(
            bst.at[lax.rem(h, slots), :, :, slan], o_block.at[h, :, mine, :], b_ss.at[h], b_rs.at[h], sib
        )

    def igrad_local(h):
        return pltpu.make_async_copy(igst.at[lax.rem(h, slots), :, :, clan], o_igrad.at[h, :, mine, :], g_loc.at[h])

    def igrad_send(h):
        return remote(
            igst.at[lax.rem(h, slots), :, :, slan], o_igrad.at[h, :, mine, :], g_ss.at[h], g_rs.at[h], sib
        )

    def s3_copy(h):
        return remote(s3.at[h], r3.at[h], ss3.at[h], rs3.at[h], xn)

    loads[1].wait()

    def expand_row(h, carry):
        for s in row_loads(h):
            s.wait()

        @pl.when(h >= slots)
        def _():
            block_local(h - slots).wait()
            block_send(h - slots).wait_send()

        pre = preE[h]
        out = pre * gain + bias
        bst[lax.rem(h, slots)] = (imgb[h].astype(F32) + out * scaled_gate).astype(BF16)
        block_local(h).start()
        block_send(h).start()
        grad = ogb[h].astype(F32) * scaled_gate + pool_part
        piece = (grad * gain).astype(BF16).reshape(W * NI, CH)
        gpe[h] = piece.reshape(W, NI, CH)
        s3[h] = dot_nt(piece, ke[olan, :]).astype(BF16).reshape(W, NI, MH)
        s3_copy(h).start()
        preE[h, :, :, 0:MH] = dot_nt(piece, ke[mlan, :]).reshape(W, NI, MH)
        return carry

    lax.fori_loop(0, H, expand_row, 0)

    loads[6].wait()
    step = 128

    def expand_kernel_grad(j, carry):
        lanes = pl.ds(pl.multiple_of(j * step, step), step)
        left = as2[:, :, :, lanes].reshape(H * W * NI, step)
        o_De[lanes, :] = dot_tn(left, gpe[...].reshape(H * W * NI, CH)).astype(BF16)
        return carry

    lax.fori_loop(0, M // step, expand_kernel_grad, 0)

    for k in (9, 5, 3, 8, 4, 2, 7, 0):
        loads[k].wait()
    turned = jnp.broadcast_to((asp[ci] > 0.5)[None], (W, NI, G))
    reduce_gain, reduce_bias = mvec[xi, 0:1], mvec[xi, 1:2]
    first_gain, first_bias = mvec[xi, 2:3], mvec[xi, 3:4]
    second_gain, second_bias = mvec[xi, 4:5], mvec[xi, 5:6]

    def s4_copy(h):
        return remote(gpr.at[h, :, :, mlan], gpr.at[h, :, :, mlan], ss4.at[h], rs4.at[h], xn)

    def s4_arrival(h):
        return remote(gpr.at[h, :, :, olan], gpr.at[h, :, :, olan], ss4.at[h], rs4.at[h], xn)

    def tally(row, grad, pre):
        flat = (grad * pre).reshape(W * NI, MH)
        o_sum[row : row + 1, :] += jnp.sum(flat, axis=0, keepdims=True)
        o_sum[row + 1 : row + 2, :] += jnp.sum(grad.reshape(W * NI, MH), axis=0, keepdims=True)

    def wave(t, carry):
        @pl.when(t < H)
        def _():
            s3_copy(t).wait_recv()
            cot = (preE[t, :, :, 0:MH] + r3[t].astype(F32)).astype(BF16).astype(F32)
            pre = preS[t]
            grad = cot * (GELU_SCALE * gelu_slope(pre * second_gain + second_bias))
            tally(4, grad, pre)
            GS[t + 1, 1 : W + 1] = (grad * second_gain).astype(BF16)

        @pl.when((t >= 1) & (t <= H))
        def _():
            cot = conv_row(GS, t - 1, kt2, turned, W, G)
            pre = preF[t - 1]
            grad = cot * (GELU_SCALE * gelu_slope(pre * first_gain + first_bias))
            tally(2, grad, pre)
            GF[t, 1 : W + 1] = (grad * first_gain).astype(BF16)

        @pl.when((t >= 2) & (t <= H + 1))
        def _():
            cot = conv_row(GF, t - 2, kt1, turned, W, G)
            pre = preR[t - 2]
            grad = cot * (GELU_SCALE * gelu_slope(pre * reduce_gain + reduce_bias))
            tally(0, grad, pre)
            gpr[t - 2, :, :, mlan] = (grad * reduce_gain).astype(BF16)
            s4_copy(t - 2).start()

        @pl.when(t >= LAG)
        def _():
            h = t - LAG
            s4_arrival(h).wait_recv()

            @pl.when(h >= slots)
            def _():
                igrad_local(h - slots).wait()
                igrad_send(h - slots).wait_send()

            rows = dot_nt(gpr[h].reshape(W * NI, M), kr[...]).reshape(W, NI, CH)
            igst[lax.rem(h, slots)] = ogb[h].astype(F32) + INV_BETA * rows
            igrad_local(h).start()
            igrad_send(h).start()

        return carry

    lax.fori_loop(0, H + LAG, wave, 0)

    for act, cot, dst in ((PF, GS, o_D2), (PR, GF, o_D1)):
        for g in range(MH // G):
            total = None
            for part in range(2):
                first = part * (H // 2)

                def fill(h, carry):
                    at = pl.ds(pl.multiple_of(h * (W * NI), W * NI), W * NI)
                    pbuf[at, :] = patches(act, first + h, g, turned, W, G)
                    return carry

                lax.fori_loop(0, H // 2, fill, 0)
                right = cot[1 + first : 1 + first + H // 2, 1 : W + 1, :, g * G : (g + 1) * G]
                term = dot_tn(right.reshape(H // 2 * W * NI, G), pbuf[...])
                total = term if total is None else total + term
            dst[g * G : (g + 1) * G, :] = total.astype(BF16)

    def reduce_kernel_grad(j, carry):
        lanes = pl.ds(pl.multiple_of(j * step, step), step)
        left = (imgb[:, :, :, lanes].astype(F32) * INV_BETA).astype(BF16).reshape(H * W * NI, step)
        o_Dr[lanes, :] = dot_tn(left, gpr[...].reshape(H * W * NI, M)).astype(BF16)
        return carry

    lax.fori_loop(0, CH // step, reduce_kernel_grad, 0)

    def drain(h, carry):
        s3_copy(h).wait_send()
        s4_copy(h).wait_send()
        block_send(h).wait_recv()
        igrad_send(h).wait_recv()
        return carry

    lax.fori_loop(0, H, drain, 0)
    for h in range(H - slots, H):
        block_local(h).wait()
        block_send(h).wait_send()
        igrad_local(h).wait()
        igrad_send(h).wait_send()


def standard_grad(summed, centered, rate, column_sum, column_cross, fan_in):
    return rate * (summed - column_sum / fan_in) - rate * rate * rate * centered * column_cross


def standardize(weight, axes):
    middle = jnp.mean(weight, axis=axes, keepdims=True)
    centered = weight - middle
    spread = jnp.sum(centered * centered, axis=axes, keepdims=True)
    return centered * lax.rsqrt(spread + STD_EPSILON)


def body(
    images, aspect, reduce_weight, reduce_gain, reduce_bias, first_weight, first_gain, first_bias,
    second_weight, second_gain, second_bias, expand_weight, expand_gain, expand_bias, excite_down,
    excite_down_bias, excite_up, excite_up_bias, skip_gain, out_grad,
):
    N, H, W, CS = images.shape
    M = reduce_weight.shape[1]
    G = first_weight.shape[2]
    NI, MH, CH = N // 2, M // 2, 2 * CS
    dims = (H, W, NI, CS, CH, MH, M, G)
    quarter = expand_weight.shape[0]
    index = lax.axis_index("chan")
    img = jnp.transpose(images, (1, 2, 0, 3))
    og = jnp.transpose(out_grad, (1, 2, 0, 3))
    fw = first_weight.reshape(9 * G, M)
    sw = second_weight.reshape(9 * G, M)
    zero = jnp.zeros((M,), F32)
    mvec = jnp.stack([reduce_gain, reduce_bias, first_gain, first_bias, second_gain, second_bias, zero, zero])
    mvec = jnp.transpose(mvec.reshape(8, 2, MH), (1, 0, 2))
    cz = jnp.zeros((CS,), F32)
    cvec = jnp.stack(
        [expand_gain, expand_bias, excite_up_bias, jnp.broadcast_to(ALPHA_RES * skip_gain, (CS,)), cz, cz, cz, cz]
    )
    asp = jnp.broadcast_to(aspect.astype(F32).reshape(2, NI, 1), (2, NI, G))
    db = excite_down_bias.reshape(1, M)

    anyspec = pl.BlockSpec(memory_space=pl.ANY)
    vm = pl.BlockSpec(memory_space=pltpu.VMEM)
    S = jax.ShapeDtypeStruct
    V = pltpu.VMEM
    DMA = pltpu.SemaphoreType.DMA
    big = (
        S((H, W, NI, CH), F32), S((H, W, NI, CH), BF16), S((H, W, NI, CH), BF16), S((H, W, NI, M), BF16),
        S((CH, M), BF16), S((M, CH), BF16), S((H, W, NI, MH), F32), S((H, W, NI, MH), F32), S((H, W, NI, MH), F32),
        S((H + 2, W + 2, NI, MH), BF16), S((H + 2, W + 2, NI, MH), BF16), S((9 * G, MH), BF16), S((9 * G, MH), BF16),
    )
    small = (S((6, NI, CH), F32), S((8, CH), F32), S((8, M), F32), S((2, 8, CH), F32), S((8, CH), F32))
    fwd = pl.pallas_call(
        functools.partial(forward_kernel, dims),
        name="forward",
        out_shape=big + small,
        in_specs=[anyspec] * 8 + [vm, anyspec, vm, vm],
        out_specs=[anyspec] * 13 + [vm] * 5,
        scratch_shapes=[
            V((H, W, NI, CH), BF16), V((H, W, NI, CH), BF16), V((CH, M), BF16), V((4, quarter, CH), BF16),
            V((CH, M), BF16), V((M, CH), BF16), V((9 * G, MH), BF16), V((9 * G, MH), BF16), V((4, 8, M), F32),
            V((CH, M), BF16), V((M, CH), BF16), V((9 * G, MH), BF16), V((9 * G, MH), BF16), V((9 * G, MH), BF16),
            V((9 * G, MH), BF16),
            V((H, W, NI, MH), F32), V((H, W, NI, MH), BF16), V((H, W, NI, MH), BF16),
            V((H + 2, W + 2, NI, MH), BF16), V((H + 2, W + 2, NI, MH), BF16),
            V((H, W, NI, MH), F32), V((H, W, NI, MH), F32), V((H, W, NI, M), BF16), V((H, W, NI, CH), F32),
            V((3, NI, CH), F32), V((2, NI, M), F32), V((2, NI, M), F32),
            DMA((H,)), DMA((H,)), DMA((H,)), DMA((8,)), DMA((8,)), DMA((8,)), DMA((3,)), DMA((4,)),
            DMA((H,)), DMA((H,)), DMA((H,)), DMA((H,)), DMA((3,)), DMA((3,)), DMA((13,)),
        ],
        compiler_params=pltpu.CompilerParams(collective_id=0, has_side_effects=True, vmem_limit_bytes=62 << 20),
    )(img, og, reduce_weight, expand_weight, excite_down, excite_up, fw, sw, mvec, cvec, db, asp)
    saved, (se, fsum, stat_r, stat_e, vb) = fwd[:13], fwd[13:]

    slots = 2
    block_out, images_grad, De, Dr, D1, D2, bsum = pl.pallas_call(
        functools.partial(backward_kernel, dims),
        name="backward",
        out_shape=(
            S((H, W, N, CS), BF16), S((H, W, N, CS), F32), S((M, CH), BF16), S((CH, M), BF16),
            S((MH, 9 * G), BF16), S((MH, 9 * G), BF16), S((8, MH), F32),
        ),
        in_specs=[anyspec] * 13 + [vm] * 4,
        out_specs=[anyspec] * 2 + [vm] * 5,
        scratch_shapes=[
            V((H, W, NI, CH), F32), V((H, W, NI, CH), BF16), V((H, W, NI, CH), BF16), V((H, W, NI, M), BF16),
            V((CH, M), BF16), V((M, CH), BF16), V((H, W, NI, MH), F32), V((H, W, NI, MH), F32), V((H, W, NI, MH), F32),
            V((H + 2, W + 2, NI, MH), BF16), V((H + 2, W + 2, NI, MH), BF16), V((9 * G, MH), BF16), V((9 * G, MH), BF16),
            V((H, W, NI, CH), BF16), V((H, W, NI, MH), BF16), V((H, W, NI, MH), BF16),
            V((H + 2, W + 2, NI, MH), BF16), V((H + 2, W + 2, NI, MH), BF16), V((H, W, NI, M), BF16),
            V((slots, W, NI, CH), BF16), V((slots, W, NI, CH), F32), V((H // 2 * W * NI, 9 * G), BF16),
            DMA((10,)), DMA((H, 3)), DMA((H,)), DMA((H,)), DMA((H,)), DMA((H,)),
            DMA((H,)), DMA((H,)), DMA((H,)), DMA((H,)), DMA((H,)), DMA((H,)),
        ],
        compiler_params=pltpu.CompilerParams(collective_id=1, has_side_effects=True, vmem_limit_bytes=63 << 20),
    )(*saved, se, vb, mvec, asp)

    xi, ci = index // 2, index % 2
    both = ("dp", "chan")
    def put(v, at, length, axis):
        shape = list(v.shape)
        shape[axis] = length
        return lax.dynamic_update_slice_in_dim(jnp.zeros(shape, v.dtype), v, at, axis)

    Dr, De, D1, D2 = (v.astype(F32) for v in (Dr, De, D1, D2))
    dr_all = lax.psum(put(Dr, xi * CH, 2 * CH, 0), both)
    de_all = lax.psum(put(De, xi * CH, 2 * CH, 1), both)
    d12 = lax.psum(put(jnp.stack([D1, D2]), xi * MH, M, 1), both)
    bs = lax.psum(put(bsum, xi * MH, M, 1), both)
    fs = lax.psum(put(fsum, xi * CH, 2 * CH, 1), both)
    ddown = lax.psum(put(jnp.dot(se[2].T, se[3], precision=lax.Precision.HIGHEST), xi * CH, 2 * CH, 0), both)
    dup = lax.psum(put(jnp.dot(se[4].T, se[5], precision=lax.Precision.HIGHEST), xi * CH, 2 * CH, 1), both)

    fan_r = 4 * CS
    r_mean, r_rate = stat_r[0:1], stat_r[1:2]
    own_rows = reduce_weight.astype(F32) - r_mean
    raw_all = lax.all_gather(reduce_weight, "chan", axis=0, tiled=True).astype(F32) - r_mean
    r_sum = jnp.sum(dr_all, axis=0, keepdims=True)
    r_cross = jnp.sum(dr_all * raw_all, axis=0, keepdims=True)
    my_dr = lax.dynamic_slice_in_dim(dr_all, index * CS, CS, 0)
    reduce_weight_grad = standard_grad(my_dr, own_rows, r_rate, r_sum, r_cross, fan_r)
    e_mean = jnp.concatenate([stat_e[0, 0:1], stat_e[1, 0:1]], axis=1)
    e_rate = jnp.concatenate([stat_e[0, 1:2], stat_e[1, 1:2]], axis=1)
    e_own = expand_weight.astype(F32) - e_mean
    e_all = lax.all_gather(expand_weight, "chan", axis=0, tiled=True).astype(F32) - e_mean
    e_sum = jnp.sum(de_all, axis=0, keepdims=True)
    e_cross = jnp.sum(de_all * e_all, axis=0, keepdims=True)
    my_de = lax.dynamic_slice_in_dim(de_all, index * quarter, quarter, 0)
    expand_weight_grad = standard_grad(my_de, e_own, e_rate, e_sum, e_cross, 4 * quarter)
    def group_grad(weight, dt):
        total = jnp.transpose(dt).reshape(3, 3, G, M)
        _, pull = jax.vjp(lambda w: standardize(w, (0, 1, 2)), weight.astype(F32))
        return pull(total)[0]

    first_weight_grad = group_grad(first_weight, d12[0])
    second_weight_grad = group_grad(second_weight, d12[1])
    my = lambda v: lax.dynamic_slice_in_dim(v, index * CS, CS, 0)
    back = lambda v: jnp.transpose(v, (2, 0, 1, 3))
    return (
        back(block_out), back(images_grad), reduce_weight_grad, bs[0], bs[1], first_weight_grad, bs[2], bs[3],
        second_weight_grad, bs[4], bs[5], expand_weight_grad, my(fs[0]), my(fs[1]),
        lax.dynamic_slice_in_dim(ddown, index * CS, CS, 0), fs[4][:M], lax.dynamic_slice_in_dim(dup, index * CS, CS, 1),
        my(fs[2]), jnp.sum(fs[3]).reshape(1),
    )


def solution(mesh):
    rows = P("dp", None, None, "chan")
    placed = (
        rows, P("dp"), P("chan", None), P(), P(), P(), P(), P(), P(), P(), P(), P("chan", None), P("chan"), P("chan"),
        P("chan", None), P(), P(None, "chan"), P("chan"), P(), rows,
    )
    results = (
        rows, rows, P("chan", None), P(), P(), P(), P(), P(), P(), P(), P(), P("chan", None), P("chan"), P("chan"),
        P("chan", None), P(), P(None, "chan"), P("chan"), P(),
    )
    return jax.shard_map(body, mesh=mesh, in_specs=placed, out_specs=results, check_vma=False)
```

```python
import functools
import jax
import jax.numpy as jnp
from jax import lax
from jax.experimental import pallas as pl
from jax.experimental.pallas import tpu as pltpu
from jax.sharding import PartitionSpec as P

INV_BETA = 1.0 / 1.16619037896906
ALPHA_RES = 0.2
GELU_SCALE = 1.7015
STD_EPSILON = 0.0001
ROOT = 0.7978845608028654
CUBIC = 0.044715
MESH = pl.DeviceIdType.MESH
F32 = jnp.float32
BF16 = jnp.bfloat16
LAG = 5


def gelu(v):
    return 0.5 * v * (1.0 + jnp.tanh(ROOT * v * (1.0 + CUBIC * v * v)))


def gelu_slope(v):
    square = v * v
    t = jnp.tanh(ROOT * v * (1.0 + CUBIC * square))
    return 0.5 * (1.0 + t) + 0.5 * v * (1.0 - t * t) * ROOT * (1.0 + 3.0 * CUBIC * square)


def split3(x):
    high = x.astype(BF16)
    rest = x - high.astype(F32)
    middle = rest.astype(BF16)
    low = (rest - middle.astype(F32)).astype(BF16)
    return jnp.concatenate([high, middle, low], axis=0)


def dot3(x, w, over):
    rows = x.shape[0]
    y = lax.dot_general(split3(x), w, (((1,), (over,)), ((), ())), preferred_element_type=F32)
    return y[:rows] + y[rows : 2 * rows] + y[2 * rows :]


def dot_nt(x, w):
    return lax.dot_general(x, w, (((1,), (1,)), ((), ())), preferred_element_type=F32)


def dot_tn(x, y):
    return lax.dot_general(x, y, (((0,), (0,)), ((), ())), preferred_element_type=F32)


def place():
    d, c = lax.axis_index("dp"), lax.axis_index("chan")
    xi, ci = c // 2, c % 2
    sib = (d, xi * 2 + (1 - ci))
    xn = (d, (1 - xi) * 2 + ci)
    dg = (d, (1 - xi) * 2 + (1 - ci))
    return d, c, xi, ci, sib, xn, dg


def greet(peers):
    barrier = pltpu.get_barrier_semaphore()
    for peer in peers:
        pl.semaphore_signal(barrier, inc=1, device_id=peer, device_id_type=MESH)
    pl.semaphore_wait(barrier, len(peers))


def remote(src, dst, send, recv, peer):
    return pltpu.make_async_remote_copy(
        src_ref=src, dst_ref=dst, send_sem=send, recv_sem=recv, device_id=peer, device_id_type=MESH
    )


def patches(ref, h, group, turned, width, taps):
    lanes = slice(group * taps, (group + 1) * taps)
    shifted = [[ref[h + u, v : v + width, :, lanes] for v in range(3)] for u in range(3)]
    parts = []
    for u in range(3):
        for v in range(3):
            if u == v:
                parts.append(shifted[u][v])
            else:
                parts.append(jnp.where(turned, shifted[v][u], shifted[u][v]))
    whole = jnp.concatenate(parts, axis=-1)
    return whole.reshape(whole.shape[0] * whole.shape[1], whole.shape[2])


def conv_row(ref, h, kernel_ref, turned, width, taps):
    groups = kernel_ref.shape[1] // taps
    outs = []
    for g in range(groups):
        outs.append(
            jnp.dot(
                patches(ref, h, g, turned, width, taps),
                kernel_ref[:, g * taps : (g + 1) * taps],
                preferred_element_type=F32,
            )
        )
    whole = jnp.concatenate(outs, axis=-1)
    return whole.reshape(width, -1, whole.shape[-1])


def forward_kernel(
    dims,
    img, og, rw, ew, dn, up, fw, sw, mvec, cvec, db, asp,
    o_preE, o_og, o_img, o_as2, o_kr, o_ke, o_preR, o_preF, o_preS, o_PR, o_PF, o_kt1, o_kt2,
    o_kraw, o_ewb, o_rawt, o_fac, o_se, o_sum, o_str, o_ste, o_vb,
    imgb, ogb, kraw, ewb, dnb, upb, fraw, sraw, st, kr, ke, k1, k2, kt1, kt2, rawt, fac,
    preR, s1, r1, PR, PF, preF, preS, as2, preE, acc, px, hx,
    loc_img, ss_img, rs_img, loc, ss, rs, ss_st, rs_st, ss1, rs1, ss2, rs2, sx, rx, outs,
):
    H, W, NI, CS, CH, MH, M, G = dims
    d, c, xi, ci, sib, xn, dg = place()
    greet((sib, xn, dg))
    mine = pl.ds(pl.multiple_of(ci * NI, NI), NI)
    theirs = pl.ds(pl.multiple_of((1 - ci) * NI, NI), NI)
    clan = pl.ds(pl.multiple_of(ci * CS, CS), CS)
    mlan = pl.ds(pl.multiple_of(xi * MH, MH), MH)
    olan = pl.ds(pl.multiple_of((1 - xi) * MH, MH), MH)

    def img_send(h):
        return remote(img.at[h, :, theirs, :], imgb.at[h, :, :, clan], ss_img.at[h], rs_img.at[h], sib)

    def img_local(h):
        return pltpu.make_async_copy(img.at[h, :, mine, :], imgb.at[h, :, :, clan], loc_img.at[h])

    locals_ = [
        pltpu.make_async_copy(rw, kraw.at[clan, :], loc.at[0]),
        pltpu.make_async_copy(ew.at[:, pl.ds(pl.multiple_of(xi * CH, CH), CH)], ewb.at[c], loc.at[1]),
        pltpu.make_async_copy(dn, dnb.at[clan, :], loc.at[2]),
        pltpu.make_async_copy(up, upb.at[:, clan], loc.at[3]),
        pltpu.make_async_copy(fw.at[:, mlan], fraw, loc.at[4]),
        pltpu.make_async_copy(sw.at[:, mlan], sraw, loc.at[5]),
        pltpu.make_async_copy(cvec, o_vb.at[:, clan], loc.at[6]),
        pltpu.make_async_copy(og.at[:, :, mine, :], ogb.at[:, :, :, clan], loc.at[7]),
    ]
    sends = [
        remote(rw, kraw.at[clan, :], ss.at[0], rs.at[0], sib),
        remote(ew.at[:, pl.ds(pl.multiple_of(xi * CH, CH), CH)], ewb.at[c], ss.at[1], rs.at[1], sib),
        remote(dn, dnb.at[clan, :], ss.at[2], rs.at[2], sib),
        remote(up, upb.at[:, clan], ss.at[3], rs.at[3], sib),
        remote(cvec, o_vb.at[:, clan], ss.at[4], rs.at[4], sib),
        remote(og.at[:, :, theirs, :], ogb.at[:, :, :, clan], ss.at[5], rs.at[5], sib),
        remote(ew.at[:, pl.ds(pl.multiple_of((1 - xi) * CH, CH), CH)], ewb.at[c], ss.at[6], rs.at[6], xn),
        remote(ew.at[:, pl.ds(pl.multiple_of((1 - xi) * CH, CH), CH)], ewb.at[c], ss.at[7], rs.at[7], dg),
    ]
    locals_[0].start()
    sends[0].start()

    def start_img(h, carry):
        img_local(h).start()
        img_send(h).start()
        return carry

    lax.fori_loop(0, H, start_img, 0)
    for k in (4, 5, 1, 6, 2, 3, 7):
        locals_[k].start()

    locals_[0].wait()
    own = kraw[clan, :].astype(F32)
    middle = jnp.mean(own, axis=0, keepdims=True)
    away = own - middle
    st[c] = jnp.concatenate(
        [middle, jnp.sum(away * away, axis=0, keepdims=True), jnp.zeros((6, M), F32)], axis=0
    )
    stats = [remote(st.at[c], st.at[c], ss_st.at[k], rs_st.at[c], peer) for k, peer in enumerate((sib, xn, dg))]
    for s in stats:
        s.start()
    for k in (6, 7, 1, 4, 2, 3, 5):
        sends[k].start()

    edge_w = jnp.zeros((W + 2, NI, MH), BF16)
    for ref in (PR, PF):
        ref[0] = edge_w
        ref[H + 1] = edge_w
        for h in range(1, H + 1):
            ref[h, 0] = edge_w[0]
            ref[h, W + 1] = edge_w[0]
    acc[...] = jnp.zeros_like(acc)

    def stat_of(q):
        return remote(st.at[q], st.at[q], ss_st.at[0], rs_st.at[q], sib)

    for k in (1, 2, 3):
        stat_of(lax.rem(c + k, 4)).wait_recv()
    count = CS
    mean = (st[0, 0:1] + st[1, 0:1] + st[2, 0:1] + st[3, 0:1]) * 0.25
    spread = jnp.zeros_like(mean)
    for q in range(4):
        gap = st[q, 0:1] - mean
        spread = spread + st[q, 1:2] + count * gap * gap
    rate = lax.rsqrt(spread + STD_EPSILON)
    o_str[...] = jnp.concatenate([mean, rate, jnp.zeros((6, M), F32)], axis=0)
    sends[0].wait_recv()

    def kr_block(j, carry):
        rows = pl.ds(pl.multiple_of(j * 128, 128), 128)
        kr[rows, :] = ((kraw[rows, :].astype(F32) - mean) * rate).astype(BF16)
        return carry

    lax.fori_loop(0, CH // 128, kr_block, 0)

    def s1_copy(h):
        return remote(s1.at[h], r1.at[h], ss1.at[h], rs1.at[h], xn)

    def reduce_row(h, carry):
        img_local(h).wait()
        img_send(h).wait_recv()
        scaled = (imgb[h].astype(F32) * INV_BETA).astype(BF16).reshape(W * NI, CH)
        s1[h] = (
            jnp.dot(scaled, kr[:, olan], preferred_element_type=F32).astype(BF16).reshape(W, NI, MH)
        )
        s1_copy(h).start()
        preR[h] = jnp.dot(scaled, kr[:, mlan], preferred_element_type=F32).reshape(W, NI, MH)
        return carry

    lax.fori_loop(0, H, reduce_row, 0)

    for k, raw, kern, trans, flip in ((4, fraw, k1, kt1, rawt.at[0]), (5, sraw, k2, kt2, rawt.at[1])):
        locals_[k].wait()
        for g in range(MH // G):
            lanes = slice(g * G, (g + 1) * G)
            w = raw[:, lanes].astype(F32)
            w = w - jnp.mean(w, axis=0, keepdims=True)
            w = w * lax.rsqrt(jnp.sum(w * w, axis=0, keepdims=True) + STD_EPSILON)
            kern[:, lanes] = w.astype(BF16)
            for tap in range(9):
                block = kern[(8 - tap) * G : (9 - tap) * G, lanes].astype(F32)
                trans[tap * G : (tap + 1) * G, lanes] = block.T.astype(BF16)
                block = raw[tap * G : (tap + 1) * G, lanes].astype(F32)
                flip[lanes, tap * G : (tap + 1) * G] = block.T.astype(BF16)

    locals_[1].wait()
    for k, peer in ((1, sib), (6, xn), (7, dg)):
        q = peer[1]
        remote(ewb.at[q], ewb.at[q], ss.at[k], rs.at[k], peer).wait_recv()
    quarter = ewb.shape[1]
    e_stat = []
    for j in range(CH // 128):
        lanes = slice(j * 128, (j + 1) * 128)
        blocks = [ewb[q, :, lanes].astype(F32) for q in range(4)]
        total = sum(jnp.sum(b, axis=0, keepdims=True) for b in blocks)
        e_mean = total / (4 * quarter)
        blocks = [b - e_mean for b in blocks]
        squares = sum(jnp.sum(b * b, axis=0, keepdims=True) for b in blocks)
        e_rate = lax.rsqrt(squares + STD_EPSILON)
        for q in range(4):
            ke[q * quarter : (q + 1) * quarter, lanes] = (blocks[q] * e_rate).astype(BF16)
        e_stat.append(jnp.concatenate([e_mean, e_rate, jnp.zeros((6, 128), F32)], axis=0))
    o_ste[xi] = jnp.concatenate(e_stat, axis=-1)
    ste_copy = remote(o_ste.at[xi], o_ste.at[xi], sx.at[2], rx.at[2], xn)
    ste_copy.start()

    turned = jnp.broadcast_to((asp[ci] > 0.5)[None], (W, NI, G))
    reduce_gain, reduce_bias = mvec[xi, 0:1], mvec[xi, 1:2]
    first_gain, first_bias = mvec[xi, 2:3], mvec[xi, 3:4]
    second_gain, second_bias = mvec[xi, 4:5], mvec[xi, 5:6]

    locals_[7].wait()
    sends[5].wait_recv()

    def s2_copy(h):
        return remote(as2.at[h, :, :, mlan], as2.at[h, :, :, mlan], ss2.at[h], rs2.at[h], xn)

    def s2_arrival(h):
        return remote(as2.at[h, :, :, olan], as2.at[h, :, :, olan], ss2.at[h], rs2.at[h], xn)

    def wave(t, carry):
        @pl.when(t < H)
        def _():
            s1_copy(t).wait_recv()
            pre = preR[t] + r1[t].astype(F32)
            preR[t] = pre
            PR[t + 1, 1 : W + 1] = (GELU_SCALE * gelu(pre * reduce_gain + reduce_bias)).astype(BF16)

        @pl.when((t >= 1) & (t <= H))
        def _():
            pre = conv_row(PR, t - 1, k1, turned, W, G)
            preF[t - 1] = pre
            PF[t, 1 : W + 1] = (GELU_SCALE * gelu(pre * first_gain + first_bias)).astype(BF16)

        @pl.when((t >= 2) & (t <= H + 1))
        def _():
            pre = conv_row(PF, t - 2, k2, turned, W, G)
            preS[t - 2] = pre
            as2[t - 2, :, :, mlan] = (GELU_SCALE * gelu(pre * second_gain + second_bias)).astype(BF16)
            s2_copy(t - 2).start()

        @pl.when(t >= LAG)
        def _():
            h = t - LAG
            s2_arrival(h).wait_recv()
            pre = jnp.dot(as2[h].reshape(W * NI, M), ke[...], preferred_element_type=F32).reshape(W, NI, CH)
            preE[h] = pre
            grad = ogb[h].astype(F32)
            acc[0] += jnp.sum(pre, axis=0)
            acc[1] += jnp.sum(grad, axis=0)
            acc[2] += jnp.sum(grad * pre, axis=0)

        return carry

    lax.fori_loop(0, H + LAG, wave, 0)

    pairs = (
        (preE, o_preE), (ogb, o_og), (imgb, o_img), (as2, o_as2), (kr, o_kr), (ke, o_ke), (preR, o_preR),
        (preF, o_preF), (preS, o_preS), (PR, o_PR), (PF, o_PF), (kt1, o_kt1), (kt2, o_kt2),
        (kraw, o_kraw), (ewb, o_ewb), (rawt, o_rawt),
    )
    saves = [pltpu.make_async_copy(a, b, outs.at[k]) for k, (a, b) in enumerate(pairs)]
    for s in saves:
        s.start()

    for k in (2, 3, 6):
        locals_[k].wait()
    for k in (2, 3, 4):
        sends[k].wait_recv()
    gain, bias = o_vb[0:1, :], o_vb[1:2, :]
    up_bias, branch_scale = o_vb[2:3, :], o_vb[3:4, :]
    pixels = H * W
    sum_pre, sum_grad, sum_both = acc[0], acc[1], acc[2]
    pooled = gain * (sum_pre * (1.0 / pixels)) + bias
    px[xi] = dot3(pooled, dnb[...], 0)
    p_copy = remote(px.at[xi], px.at[xi], sx.at[0], rx.at[0], xn)
    p_copy.start()
    remote(px.at[1 - xi], px.at[1 - xi], sx.at[0], rx.at[0], xn).wait_recv()
    down = px[0] + px[1] + db[...]
    hidden = gelu(down)
    upper = dot3(hidden, upb[...], 0) + up_bias
    sigma = 1.0 / (1.0 + jnp.exp(-upper))
    gating = 2.0 * sigma
    grad_gating_raw = gain * sum_both + bias * sum_grad
    grad_upper = branch_scale * grad_gating_raw * 2.0 * sigma * (1.0 - sigma)
    hx[xi] = dot3(grad_upper, upb[...], 1)
    h_copy = remote(hx.at[xi], hx.at[xi], sx.at[1], rx.at[1], xn)
    h_copy.start()
    remote(hx.at[1 - xi], hx.at[1 - xi], sx.at[1], rx.at[1], xn).wait_recv()
    grad_down = (hx[0] + hx[1]) * gelu_slope(down)
    grad_pooled = dot3(grad_down, dnb[...], 1)
    scaled_gate = branch_scale * gating
    pool_part = grad_pooled * (1.0 / pixels)
    o_se[0] = scaled_gate
    o_se[1] = pool_part
    for s in range(2):
        shard = slice(s * CS, (s + 1) * CS)
        fac[s] = jnp.concatenate([pooled[:, shard], grad_down, hidden, grad_upper[:, shard]], axis=-1).astype(BF16)
    fac_save = pltpu.make_async_copy(fac, o_fac, outs.at[16])
    fac_save.start()
    gain_grad = jnp.sum(scaled_gate * sum_both + pool_part * sum_pre, axis=0, keepdims=True)
    bias_grad = jnp.sum(scaled_gate * sum_grad + grad_pooled, axis=0, keepdims=True)
    up_bias_grad = jnp.sum(grad_upper, axis=0, keepdims=True)
    skip_row = ALPHA_RES * jnp.sum(gating * grad_gating_raw, axis=0, keepdims=True)
    down_bias_grad = jnp.sum(grad_down, axis=0, keepdims=True)
    o_sum[...] = jnp.concatenate(
        [gain_grad, bias_grad, up_bias_grad, skip_row, down_bias_grad, jnp.zeros((3, CH), F32)], axis=0
    )

    remote(o_ste.at[1 - xi], o_ste.at[1 - xi], sx.at[2], rx.at[2], xn).wait_recv()
    for s in (ste_copy, p_copy, h_copy):
        s.wait_send()
    for s in sends + stats:
        s.wait_send()

    def drain(h, carry):
        img_send(h).wait_send()
        s1_copy(h).wait_send()
        s2_copy(h).wait_send()
        return carry

    lax.fori_loop(0, H, drain, 0)
    for s in saves:
        s.wait()
    fac_save.wait()


class DeviceSum:
    def __init__(self, where, block, rows, sbuf, ysend, ybuf, zsend, zbuf, s_ss, s_rs, y_ss, y_rs, z_ss, z_rs):
        self.ci, self.yb, self.zz, self.sib, self.yp, self.zpeer, self.zb = where
        self.block, self.rows = block, rows
        self.sbuf, self.ysend, self.ybuf, self.zsend, self.zbuf = sbuf, ysend, ybuf, zsend, zbuf
        self.s_ss, self.s_rs, self.y_ss, self.y_rs, self.z_ss, self.z_rs = s_ss, s_rs, y_ss, y_rs, z_ss, z_rs
        self.count = sbuf.shape[0]
        self.half = rows // 2

    def core_copy(self, b):
        ref, base = self.block(b, 1 - self.ci)
        src = ref.at[pl.ds(pl.multiple_of(base, 16), self.rows), :]
        return remote(src, self.sbuf.at[b], self.s_ss.at[b], self.s_rs.at[b], self.sib)

    def y_copy(self):
        return remote(self.ysend, self.ybuf, self.y_ss.at[0], self.y_rs.at[0], self.yp)

    def z_copy(self, k):
        to, peer = self.zpeer(k)
        return remote(self.zsend.at[to], self.zbuf.at[self.zz], self.z_ss.at[k], self.z_rs.at[self.zz], peer)

    def z_arrival(self, k):
        to, peer = self.zpeer(k)
        return remote(self.zsend.at[to], self.zbuf.at[to], self.z_ss.at[k], self.z_rs.at[to], peer)

    def core_sum(self, b, y):
        ref, base = self.block(b, self.ci)
        at = pl.multiple_of(y * self.half, 16)
        mine = ref[pl.ds(pl.multiple_of(base + at, 16), self.half), :]
        return mine.astype(F32) + self.sbuf[b, pl.ds(at, self.half), :].astype(F32)

    def to_core(self, b):
        self.core_copy(b).start()

    def to_y(self):
        for b in range(self.count):
            self.core_copy(b).wait_recv()
        for b in range(self.count):
            self.ysend[b] = self.core_sum(b, 1 - self.yb).astype(BF16)
        self.y_copy().start()

    def to_z(self):
        self.y_copy().wait_recv()
        piece = self.half // self.zb
        for b in range(self.count):
            total = self.core_sum(b, self.yb) + self.ybuf[b].astype(F32)
            for z in range(self.zb):
                self.zsend[z, b] = total[z * piece : (z + 1) * piece].astype(BF16)
        for k in range(1, self.zb):
            self.z_copy(k).start()

    def totals(self):
        for k in range(1, self.zb):
            self.z_arrival(k).wait_recv()
        outs = []
        for b in range(self.count):
            total = self.zsend[self.zz, b].astype(F32)
            for k in range(1, self.zb):
                total = total + self.zbuf[self.zpeer(k)[0], b].astype(F32)
            outs.append(total)
        return outs

    def finish(self, cores=True):
        if cores:
            for b in range(self.count):
                self.core_copy(b).wait_send()
        self.y_copy().wait_send()
        for k in range(1, self.zb):
            self.z_copy(k).wait_send()


class Spread:
    def __init__(self, where, full, z_ss, z_rs, y_ss, y_rs):
        self.ci, self.yb, self.zz, self.sib, self.yp, self.zpeer, self.zb = where
        self.full = full
        self.z_ss, self.z_rs, self.y_ss, self.y_rs = z_ss, z_rs, y_ss, y_rs

    def z_copy(self, k):
        own = self.full.at[self.yb, self.zz]
        return remote(own, own, self.z_ss.at[k], self.z_rs.at[self.zz], self.zpeer(k)[1])

    def y_copy(self):
        own = self.full.at[self.yb]
        return remote(own, own, self.y_ss.at[0], self.y_rs.at[0], self.yp)

    def to_z(self):
        for k in range(1, self.zb):
            self.z_copy(k).start()

    def to_y(self):
        for k in range(1, self.zb):
            to, peer = self.zpeer(k)
            slot = self.full.at[self.yb, to]
            remote(slot, slot, self.z_ss.at[k], self.z_rs.at[to], peer).wait_recv()
        self.y_copy().start()

    def arrive(self):
        slot = self.full.at[1 - self.yb]
        remote(slot, slot, self.y_ss.at[0], self.y_rs.at[0], self.yp).wait_recv()

    def finish(self):
        for k in range(1, self.zb):
            self.z_copy(k).wait_send()
        self.y_copy().wait_send()


class VectorSum:
    def __init__(self, where, xi, xn, vs, vy, vz, vx, ss, rs, z_ss, z_rs):
        self.ci, self.yb, self.zz, self.sib, self.yp, self.zpeer, self.zb = where
        self.xi, self.xn = xi, xn
        self.vs, self.vy, self.vz, self.vx = vs, vy, vz, vx
        self.ss, self.rs, self.z_ss, self.z_rs = ss, rs, z_ss, z_rs

    def pair(self, ref, slot, k, peer):
        return remote(ref.at[slot], ref.at[slot], self.ss.at[k], self.rs.at[k], peer)

    def z_pair(self, slot, k, peer):
        return remote(self.vz.at[slot], self.vz.at[slot], self.z_ss.at[k], self.z_rs.at[slot], peer)

    def to_core(self, value):
        self.vs[self.ci] = value
        self.pair(self.vs, self.ci, 0, self.sib).start()

    def to_y(self):
        self.pair(self.vs, 1 - self.ci, 0, self.sib).wait_recv()
        self.vy[self.yb] = self.vs[0] + self.vs[1]
        self.pair(self.vy, self.yb, 1, self.yp).start()

    def to_z(self):
        self.pair(self.vy, 1 - self.yb, 1, self.yp).wait_recv()
        self.vz[self.zz] = self.vy[0] + self.vy[1]
        for k in range(1, self.zb):
            self.z_pair(self.zz, k, self.zpeer(k)[1]).start()

    def to_x(self):
        for k in range(1, self.zb):
            to, peer = self.zpeer(k)
            self.z_pair(to, k, peer).wait_recv()
        total = self.vz[0]
        for z in range(1, self.zb):
            total = total + self.vz[z]
        self.vx[self.xi] = total
        self.pair(self.vx, self.xi, 2, self.xn).start()

    def arrive(self):
        self.pair(self.vx, 1 - self.xi, 2, self.xn).wait_recv()

    def finish(self):
        self.pair(self.vs, self.ci, 0, self.sib).wait_send()
        self.pair(self.vy, self.yb, 1, self.yp).wait_send()
        for k in range(1, self.zb):
            self.z_pair(self.zz, k, self.zpeer(k)[1]).wait_send()
        self.pair(self.vx, self.xi, 2, self.xn).wait_send()


def backward_kernel(
    dims, group,
    i_preE, i_og, i_img, i_as2, i_kr, i_ke, i_preR, i_preF, i_preS, i_PR, i_PF, i_kt1, i_kt2,
    i_kraw, i_ewb, i_rawt, i_fac, i_ew, se, fsum, str_, ste, vb, mvec, asp,
    o_block, o_igrad, o_G, o_rw, o_ew, o_dd, o_du, va, vl,
    preE, gas, ogb, imgb, as2, kr, ke, preR, preF, preS, PR, PF, kt1, kt2, raw, rawt, ewo,
    wide, s3, r3, GS, GF, bst, Dx, D12, bsum, estat, rstat, FB,
    e_s, e_ys, e_yb, e_zs, e_zb, e_fin, e_x, e_G,
    r_s, r_ys, r_yb, r_zs, r_zb, r_G,
    d_s, d_ys, d_yb, d_zs, d_zb, d_fin,
    va_s, va_y, va_z, vl_s, vl_y, vl_z,
    ld, ldr, ldp, ss3, rs3, ss4, rs4, b_loc, b_ss, b_rs, g_loc, g_ss, g_rs,
    e_sem, e_zsem, r_sem, r_zsem, d_sem, d_zsem, v_sem, v_zsem, f_sem, f_zsem, d_ag, e_xsem, credit,
):
    H, W, NI, CS, CH, MH, M, G = dims
    YB, ZB = group
    d, c, xi, ci, sib, xn, dg = place()
    yb, zz, first = d % YB, (d // YB) % ZB, (d // (YB * ZB)) * (YB * ZB)
    yp = (first + zz * YB + (1 - yb), c)

    def zpeer(k):
        to = lax.rem(zz + k, ZB)
        return to, (first + to * YB + yb, c)

    where = (ci, yb, zz, sib, yp, zpeer, ZB)
    pairs = (
        (i_kr, kr), (i_ke, ke), (i_kt1, kt1), (i_kt2, kt2), (i_PR, PR), (i_PF, PF), (i_as2, as2),
        (i_kraw, raw), (i_ewb, raw), (i_ew, ewo),
        (i_rawt.at[0, ci, yb, zz], rawt.at[0]), (i_rawt.at[1, ci, yb, zz], rawt.at[1]),
        (i_fac.at[ci], FB.at[yb, zz, ci]),
    )
    loads = [pltpu.make_async_copy(a, b, ld.at[k]) for k, (a, b) in enumerate(pairs)]
    slots, ring = bst.shape[0], preE.shape[0]
    igst = preE
    gpe = pl.ds(0, CH)

    def row_loads(h):
        return [
            pltpu.make_async_copy(i_preE.at[h], preE.at[h % ring], ldr.at[h, 0]),
            pltpu.make_async_copy(i_og.at[h], ogb.at[h], ldr.at[h, 1]),
            pltpu.make_async_copy(i_img.at[h], imgb.at[h], ldr.at[h, 2]),
        ]

    loads[1].start()
    for h in range(ring):
        for s in row_loads(h):
            s.start()
    loads[12].start()

    def pre_load(k, h):
        src, dst = ((i_preS, preS), (i_preF, preF), (i_preR, preR))[k]
        return pltpu.make_async_copy(src.at[h], dst.at[lax.rem(h, 4)], ldp.at[h, k])

    greet((sib, xn, yp) + tuple(zpeer(k)[1] for k in range(1, ZB)))
    fac_core = remote(i_fac.at[1 - ci], FB.at[yb, zz, ci], f_sem.at[0], f_sem.at[1], sib)
    fac_core.start()
    for k in (6, 8, 5, 3, 4, 2, 0, 9, 10, 11):
        loads[k].start()

    mine = pl.ds(pl.multiple_of(ci * NI, NI), NI)
    clan = pl.ds(pl.multiple_of(ci * CS, CS), CS)
    slan = pl.ds(pl.multiple_of((1 - ci) * CS, CS), CS)
    mlan = pl.ds(pl.multiple_of(xi * MH, MH), MH)
    olan = pl.ds(pl.multiple_of((1 - xi) * MH, MH), MH)
    edge_w = jnp.zeros((W + 2, NI, MH), BF16)
    for ref in (GS, GF):
        ref[0] = edge_w
        ref[H + 1] = edge_w
        for h in range(1, H + 1):
            ref[h, 0] = edge_w[0]
            ref[h, W + 1] = edge_w[0]
    bsum[...] = jnp.zeros_like(bsum)
    estat[...] = jnp.zeros_like(estat)
    rstat[...] = jnp.zeros_like(rstat)

    gain, bias = vb[0:1, :], vb[1:2, :]
    scaled_gate, pool_part = se[0], se[1]

    def block_local(h):
        return pltpu.make_async_copy(bst.at[lax.rem(h, slots), :, :, clan], o_block.at[h, :, mine, :], b_loc.at[h])

    def block_send(h):
        return remote(
            bst.at[lax.rem(h, slots), :, :, slan], o_block.at[h, :, mine, :], b_ss.at[h], b_rs.at[h], sib
        )

    def igrad_local(h):
        return pltpu.make_async_copy(igst.at[lax.rem(h, slots), :, :, clan], o_igrad.at[h, :, mine, :], g_loc.at[h])

    def igrad_send(h):
        return remote(
            igst.at[lax.rem(h, slots), :, :, slan], o_igrad.at[h, :, mine, :], g_ss.at[h], g_rs.at[h], sib
        )

    def s3_copy(h):
        return remote(s3.at[h], r3.at[h], ss3.at[h], rs3.at[h], xn)

    loads[1].wait()

    def row_load(h, k):
        src, dst = ((i_preE, preE.at[lax.rem(h, ring)]), (i_og, ogb.at[h]), (i_img, imgb.at[h]))[k]
        return pltpu.make_async_copy(src.at[h], dst, ldr.at[h, k])

    def expand_row(h, carry):
        for k in range(3):
            row_load(h, k).wait()

        @pl.when(h >= slots)
        def _():
            block_local(h - slots).wait()
            block_send(h - slots).wait_send()

        pre = preE[lax.rem(h, ring)]
        out = pre * gain + bias
        bst[lax.rem(h, slots)] = (imgb[h].astype(F32) + out * scaled_gate).astype(BF16)
        block_local(h).start()
        block_send(h).start()

        @pl.when(h + ring < H)
        def _():
            for k in range(3):
                row_load(h + ring, k).start()

        grad = ogb[h].astype(F32) * scaled_gate + pool_part
        piece = (grad * gain).astype(BF16).reshape(W * NI, CH)
        wide[pl.ds(pl.multiple_of(h * (W * NI), W * NI), W * NI), gpe] = piece
        s3[h] = dot_nt(piece, ke[olan, :]).astype(BF16).reshape(W, NI, MH)
        s3_copy(h).start()
        gas[h] = dot_nt(piece, ke[mlan, :]).reshape(W, NI, MH)
        return carry

    lax.fori_loop(0, H, expand_row, 0)
    pre_load(0, 0).start()
    pre_load(0, 1).start()
    pre_load(1, 0).start()

    loads[12].wait()
    remote(i_fac.at[1 - ci], FB.at[yb, zz, 1 - ci], f_sem.at[0], f_sem.at[1], sib).wait_recv()
    fac_spread = Spread(where, FB, f_zsem.at[0], f_zsem.at[1], f_sem.at[pl.ds(2, 1)], f_sem.at[pl.ds(3, 1)])
    fac_spread.to_z()

    loads[6].wait()
    loads[8].wait()
    quarter = ewo.shape[0]
    step = 128
    e_mean = ste[xi, 0:1, :]

    def expand_kernel_grad(j, carry):
        lanes = pl.ds(pl.multiple_of(j * step, step), step)
        left = as2[:, :, :, lanes].reshape(H * W * NI, step)
        Dx[lanes, :] = dot_tn(left, wide[:, gpe]).astype(BF16)
        return carry

    lax.fori_loop(0, M // step, expand_kernel_grad, 0)
    pl.semaphore_signal(credit, inc=1, device_id=xn, device_id_type=MESH)
    gpr = as2

    sum_e = DeviceSum(
        where, lambda b, half: (Dx, b * MH + half * quarter), quarter, e_s, e_ys, e_yb, e_zs, e_zb,
        e_sem.at[pl.ds(0, 2)], e_sem.at[pl.ds(2, 2)], e_sem.at[pl.ds(4, 1)], e_sem.at[pl.ds(5, 1)],
        e_zsem.at[0], e_zsem.at[1],
    )
    sum_e.to_core(0)
    sum_e.to_core(1)
    spread_e = Spread(where, e_G, e_zsem.at[2], e_zsem.at[3], e_sem.at[pl.ds(6, 1)], e_sem.at[pl.ds(7, 1)])

    def e_cross(slot):
        return remote(e_x.at[1 - slot], e_G.at[yb, zz, slot], e_xsem.at[0], e_xsem.at[1], xn)

    for q in range(4):
        grads = Dx[q * quarter : (q + 1) * quarter, :].astype(F32)
        away = raw[q * quarter : (q + 1) * quarter, :].astype(F32) - e_mean
        estat[0:1, :] += jnp.sum(grads, axis=0, keepdims=True)
        estat[1:2, :] += jnp.sum(grads * away, axis=0, keepdims=True)
    loads[7].start()
    sum_a = VectorSum(
        where, xi, xn, va_s, va_y, va_z, va, v_sem.at[0], v_sem.at[1], v_zsem.at[0], v_zsem.at[1]
    )
    sum_a.to_core(jnp.concatenate([fsum[0:5, :], estat[0:2, :], jnp.zeros((1, CH), F32)], axis=0))

    for k in (5, 3, 4, 2, 0):
        loads[k].wait()
    turned = jnp.broadcast_to((asp[ci] > 0.5)[None], (W, NI, G))
    reduce_gain, reduce_bias = mvec[xi, 0:1], mvec[xi, 1:2]
    first_gain, first_bias = mvec[xi, 2:3], mvec[xi, 3:4]
    second_gain, second_bias = mvec[xi, 4:5], mvec[xi, 5:6]

    def s4_copy(h):
        return remote(gpr.at[h, :, :, mlan], gpr.at[h, :, :, mlan], ss4.at[h], rs4.at[h], xn)

    def s4_arrival(h):
        return remote(gpr.at[h, :, :, olan], gpr.at[h, :, :, olan], ss4.at[h], rs4.at[h], xn)

    def tally(row, grad, pre):
        flat = (grad * pre).reshape(W * NI, MH)
        bsum[row : row + 1, :] += jnp.sum(flat, axis=0, keepdims=True)
        bsum[row + 1 : row + 2, :] += jnp.sum(grad.reshape(W * NI, MH), axis=0, keepdims=True)

    def image_row(h):
        s4_arrival(h).wait_recv()

        @pl.when(h >= slots)
        def _():
            igrad_local(h - slots).wait()
            igrad_send(h - slots).wait_send()

        rows = dot_nt(gpr[h].reshape(W * NI, M), kr[...]).reshape(W, NI, CH)
        igst[lax.rem(h, slots)] = ogb[h].astype(F32) + INV_BETA * rows
        igrad_local(h).start()
        igrad_send(h).start()

    def wave(t, carry):
        @pl.when(t + 2 < H)
        def _():
            pre_load(0, t + 2).start()

        @pl.when(t + 1 < H)
        def _():
            pre_load(1, t + 1).start()

        @pl.when(t < H)
        def _():
            pre_load(2, t).start()

        @pl.when(t < H)
        def _():
            pre_load(0, t).wait()
            s3_copy(t).wait_recv()
            cot = (gas[t] + r3[t].astype(F32)).astype(BF16).astype(F32)
            pre = preS[lax.rem(t, 4)]
            grad = cot * (GELU_SCALE * gelu_slope(pre * second_gain + second_bias))
            tally(4, grad, pre)
            GS[t + 1, 1 : W + 1] = (grad * second_gain).astype(BF16)

        @pl.when((t >= 1) & (t <= H))
        def _():
            pre_load(1, t - 1).wait()
            cot = conv_row(GS, t - 1, kt2, turned, W, G)
            pre = preF[lax.rem(t - 1, 4)]
            grad = cot * (GELU_SCALE * gelu_slope(pre * first_gain + first_bias))
            tally(2, grad, pre)
            GF[t, 1 : W + 1] = (grad * first_gain).astype(BF16)

        @pl.when(t == 2)
        def _():
            pl.semaphore_wait(credit, 1)

        @pl.when((t >= 2) & (t <= H + 1))
        def _():
            pre_load(2, t - 2).wait()
            cot = conv_row(GF, t - 2, kt1, turned, W, G)
            pre = preR[lax.rem(t - 2, 4)]
            grad = cot * (GELU_SCALE * gelu_slope(pre * reduce_gain + reduce_bias))
            tally(0, grad, pre)
            gpr[t - 2, :, :, mlan] = (grad * reduce_gain).astype(BF16)
            s4_copy(t - 2).start()

        @pl.when(t == 1)
        def _():
            fac_spread.to_y()
            sum_e.to_y()
            sum_a.to_y()

        @pl.when(t == 3)
        def _():
            sum_e.to_z()
            sum_a.to_z()

        @pl.when(t == 5)
        def _():
            fac_spread.arrive()
            sum_a.to_x()
            for b, total in enumerate(sum_e.totals()):
                e_x[b] = total.astype(BF16)
            e_G[yb, zz, xi] = e_x[xi]
            e_cross(xi).start()

        @pl.when(t == 7)
        def _():
            e_cross(1 - xi).wait_recv()
            spread_e.to_z()
            sum_a.arrive()

        @pl.when(t == 9)
        def _():
            spread_e.to_y()

        @pl.when(t >= LAG)
        def _():
            image_row(t - LAG)

        return carry

    lax.fori_loop(0, H + 2, wave, 0)

    sum_d = DeviceSum(
        where, lambda b, half: (D12.at[b], half * quarter), quarter, d_s, d_ys, d_yb, d_zs, d_zb,
        d_sem.at[pl.ds(0, 2)], d_sem.at[pl.ds(2, 2)], d_sem.at[pl.ds(4, 1)], d_sem.at[pl.ds(5, 1)],
        d_zsem.at[0], d_zsem.at[1],
    )
    for b, act, cot in ((1, PF, GS), (0, PR, GF)):
        for g in range(MH // G):
            def fill(h, carry):
                at = pl.ds(pl.multiple_of(h * (W * NI), W * NI), W * NI)
                wide[at, :] = patches(act, h, g, turned, W, G)
                return carry

            lax.fori_loop(0, H, fill, 0)
            right = cot[1 : H + 1, 1 : W + 1, :, g * G : (g + 1) * G].reshape(H * W * NI, G)
            total = dot_tn(right, wide[...])
            D12[b, g * G : (g + 1) * G, :] = total.astype(BF16)
        sum_d.to_core(b)

    for h in range(H + 2 - LAG, H):
        image_row(h)
    sum_d.to_y()

    loads[7].wait()
    for b in range(2):
        sum_e.core_copy(b).wait_send()
    r_mean, r_rate = str_[0:1, :], str_[1:2, :]

    def reduce_kernel_grad(j, carry):
        lanes = pl.ds(pl.multiple_of(j * step, step), step)
        left = (imgb[:, :, :, lanes].astype(F32) * INV_BETA).astype(BF16).reshape(H * W * NI, step)
        grads = dot_tn(left, gpr[...].reshape(H * W * NI, M))
        rstat[0:1, :] += jnp.sum(grads, axis=0, keepdims=True)
        rstat[1:2, :] += jnp.sum(grads * (raw[lanes, :].astype(F32) - r_mean), axis=0, keepdims=True)
        Dx[lanes, :] = grads.astype(BF16)
        return carry

    lax.fori_loop(0, CH // step, reduce_kernel_grad, 0)
    sum_r = DeviceSum(
        where, lambda b, half: (Dx, half * CS), CS, r_s, r_ys, r_yb, r_zs, r_zb,
        r_sem.at[pl.ds(0, 1)], r_sem.at[pl.ds(1, 1)], r_sem.at[pl.ds(2, 1)], r_sem.at[pl.ds(3, 1)],
        r_zsem.at[0], r_zsem.at[1],
    )
    spread_r = Spread(where, r_G, r_zsem.at[2], r_zsem.at[3], r_sem.at[pl.ds(4, 1)], r_sem.at[pl.ds(5, 1)])
    sum_r.to_core(0)
    sum_l = VectorSum(
        where, xi, xn, vl_s, vl_y, vl_z, vl, v_sem.at[2], v_sem.at[3], v_zsem.at[2], v_zsem.at[3]
    )
    rstat[2:8, mlan] = bsum[0:6, :]
    sum_l.to_core(rstat[...])
    sum_r.to_y()
    sum_l.to_y()
    sum_d.to_z()
    sum_r.to_z()
    sum_l.to_z()

    loads[10].wait()
    loads[11].wait()
    for b, total in enumerate(sum_d.totals()):
        weight = rawt[b].astype(F32)
        away = weight - jnp.mean(weight, axis=1, keepdims=True)
        rate = lax.rsqrt(jnp.sum(away * away, axis=1, keepdims=True) + STD_EPSILON)
        cross = jnp.sum(total * away, axis=1, keepdims=True)
        centred = total - jnp.mean(total, axis=1, keepdims=True)
        d_fin[b] = (rate * centred - rate * rate * rate * away * cross).astype(BF16)

    q = c
    qx = (1 - xi) * 2 + ci
    qs = xi * 2 + (1 - ci)
    qd = (1 - xi) * 2 + (1 - ci)
    own = o_G.at[q, yb, zz]
    d_keep = pltpu.make_async_copy(d_fin, own, d_ag.at[0])
    d_keep.start()

    def d_z(k):
        return remote(d_fin, own, d_zsem.at[2].at[k], d_zsem.at[3].at[zz], zpeer(k)[1])

    for k in range(1, ZB):
        d_z(k).start()
    for b, total in enumerate(sum_r.totals()):
        r_G[yb, zz, b] = total.astype(BF16)
    spread_r.to_z()
    sum_l.to_x()

    def d_block(quad, y, k, peer):
        ref = o_G.at[quad, y]
        return remote(ref, ref, d_ag.at[2 * k + 2], d_ag.at[2 * k + 3], peer)

    d_keep.wait()
    for k in range(1, ZB):
        to, peer = zpeer(k)
        ref = o_G.at[q, yb, to]
        remote(ref, ref, d_zsem.at[2].at[k], d_zsem.at[3].at[to], peer).wait_recv()
    d_block(q, yb, 0, yp).start()
    d_block(q, yb, 1, xn).start()
    d_block(q, yb, 2, sib).start()
    spread_r.to_y()
    d_block(q, 1 - yb, 0, yp).wait_recv()
    d_block(q, 1 - yb, 3, xn).start()
    d_block(q, 1 - yb, 4, sib).start()
    d_block(qx, yb, 1, xn).wait_recv()
    d_block(qx, yb, 5, sib).start()

    fac_all = FB[...].reshape(YB * ZB * 2 * NI, FB.shape[-1])
    o_dd[...] = dot_tn(fac_all[:, 0:CS], fac_all[:, CS : CS + M])
    o_du[...] = dot_tn(fac_all[:, CS + M : CS + 2 * M], fac_all[:, CS + 2 * M :])
    spread_e.arrive()
    loads[9].wait()
    piece = e_G.shape[3]
    for y in range(YB):
        for z in range(ZB):
            at = (y * ZB + z) * piece
            for s in range(2):
                o_ew[at : at + piece, s * CH : (s + 1) * CH] = e_G[y, z, s].astype(F32)
    fan = 1.0 / (4 * quarter)
    for s in range(2):
        lanes = slice(s * CH, (s + 1) * CH)
        mean, rate = ste[s, 0:1, :], ste[s, 1:2, :]
        low, cross = va[s, 5:6, :] * fan, va[s, 6:7, :]
        away = ewo[:, lanes].astype(F32) - mean
        o_ew[:, lanes] = rate * (o_ew[:, lanes] - low) - rate * rate * rate * away * cross
    sum_l.arrive()
    spread_r.arrive()
    low = (vl[0, 0:1, :] + vl[1, 0:1, :]) * (1.0 / (4 * CS))
    cross = vl[0, 1:2, :] + vl[1, 1:2, :]
    piece = r_G.shape[3]
    for y in range(YB):
        for z in range(ZB):
            at = (y * ZB + z) * piece
            rows = pl.ds(pl.multiple_of(ci * CS + at, 16), piece)
            away = raw[rows, :].astype(F32) - r_mean
            grads = r_G[y, z, 0].astype(F32)
            o_rw[at : at + piece, :] = r_rate * (grads - low) - r_rate * r_rate * r_rate * away * cross

    d_block(qx, 1 - yb, 3, xn).wait_recv()
    d_block(qx, 1 - yb, 6, sib).start()
    d_block(qs, yb, 2, sib).wait_recv()
    d_block(qs, 1 - yb, 4, sib).wait_recv()
    d_block(qd, yb, 5, sib).wait_recv()
    d_block(qd, 1 - yb, 6, sib).wait_recv()

    fac_core.wait_send()
    fac_spread.finish()
    e_cross(xi).wait_send()
    sum_e.finish(cores=False)
    for job in (spread_e, sum_a, sum_d, sum_r, spread_r, sum_l):
        job.finish()
    for k in range(1, ZB):
        d_z(k).wait_send()
    for k, (quad, y, peer) in enumerate(
        ((q, yb, yp), (q, yb, xn), (q, yb, sib), (q, 1 - yb, xn), (q, 1 - yb, sib), (qx, yb, sib), (qx, 1 - yb, sib))
    ):
        d_block(quad, y, k, peer).wait_send()

    def drain(h, carry):
        s3_copy(h).wait_send()
        s4_copy(h).wait_send()
        block_send(h).wait_recv()
        igrad_send(h).wait_recv()
        return carry

    lax.fori_loop(0, H, drain, 0)
    for h in range(H - slots, H):
        block_local(h).wait()
        block_send(h).wait_send()
        igrad_local(h).wait()
        igrad_send(h).wait_send()


def body(
    images, aspect, reduce_weight, reduce_gain, reduce_bias, first_weight, first_gain, first_bias,
    second_weight, second_gain, second_bias, expand_weight, expand_gain, expand_bias, excite_down,
    excite_down_bias, excite_up, excite_up_bias, skip_gain, out_grad,
):
    N, H, W, CS = images.shape
    M = reduce_weight.shape[1]
    G = first_weight.shape[2]
    NI, MH, CH = N // 2, M // 2, 2 * CS
    dims = (H, W, NI, CS, CH, MH, M, G)
    quarter = expand_weight.shape[0]
    index = lax.axis_index("chan")
    img = jnp.transpose(images, (1, 2, 0, 3))
    og = jnp.transpose(out_grad, (1, 2, 0, 3))
    fw = first_weight.reshape(9 * G, M)
    sw = second_weight.reshape(9 * G, M)
    zero = jnp.zeros((M,), F32)
    mvec = jnp.stack([reduce_gain, reduce_bias, first_gain, first_bias, second_gain, second_bias, zero, zero])
    mvec = jnp.transpose(mvec.reshape(8, 2, MH), (1, 0, 2))
    cz = jnp.zeros((CS,), F32)
    cvec = jnp.stack(
        [expand_gain, expand_bias, excite_up_bias, jnp.broadcast_to(ALPHA_RES * skip_gain, (CS,)), cz, cz, cz, cz]
    )
    asp = jnp.broadcast_to(aspect.astype(F32).reshape(2, NI, 1), (2, NI, G))
    db = excite_down_bias.reshape(1, M)

    anyspec = pl.BlockSpec(memory_space=pl.ANY)
    vm = pl.BlockSpec(memory_space=pltpu.VMEM)
    S = jax.ShapeDtypeStruct
    V = pltpu.VMEM
    DMA = pltpu.SemaphoreType.DMA
    width = 2 * CS + 2 * M
    big = (
        S((H, W, NI, CH), F32), S((H, W, NI, CH), BF16), S((H, W, NI, CH), BF16), S((H, W, NI, M), BF16),
        S((CH, M), BF16), S((M, CH), BF16), S((H, W, NI, MH), F32), S((H, W, NI, MH), F32), S((H, W, NI, MH), F32),
        S((H + 2, W + 2, NI, MH), BF16), S((H + 2, W + 2, NI, MH), BF16), S((9 * G, MH), BF16), S((9 * G, MH), BF16),
        S((CH, M), BF16), S((4, quarter, CH), BF16), S((2, MH, 9 * G), BF16), S((2, NI, width), BF16),
    )
    small = (S((2, NI, CH), F32), S((8, CH), F32), S((8, M), F32), S((2, 8, CH), F32), S((8, CH), F32))
    fwd = pl.pallas_call(
        functools.partial(forward_kernel, dims),
        name="forward",
        out_shape=big + small,
        in_specs=[anyspec] * 8 + [vm, anyspec, vm, vm],
        out_specs=[anyspec] * 17 + [vm] * 5,
        scratch_shapes=[
            V((H, W, NI, CH), BF16), V((H, W, NI, CH), BF16), V((CH, M), BF16), V((4, quarter, CH), BF16),
            V((CH, M), BF16), V((M, CH), BF16), V((9 * G, MH), BF16), V((9 * G, MH), BF16), V((4, 8, M), F32),
            V((CH, M), BF16), V((M, CH), BF16), V((9 * G, MH), BF16), V((9 * G, MH), BF16), V((9 * G, MH), BF16),
            V((9 * G, MH), BF16), V((2, MH, 9 * G), BF16), V((2, NI, width), BF16),
            V((H, W, NI, MH), F32), V((H, W, NI, MH), BF16), V((H, W, NI, MH), BF16),
            V((H + 2, W + 2, NI, MH), BF16), V((H + 2, W + 2, NI, MH), BF16),
            V((H, W, NI, MH), F32), V((H, W, NI, MH), F32), V((H, W, NI, M), BF16), V((H, W, NI, CH), F32),
            V((3, NI, CH), F32), V((2, NI, M), F32), V((2, NI, M), F32),
            DMA((H,)), DMA((H,)), DMA((H,)), DMA((8,)), DMA((8,)), DMA((8,)), DMA((3,)), DMA((4,)),
            DMA((H,)), DMA((H,)), DMA((H,)), DMA((H,)), DMA((3,)), DMA((3,)), DMA((17,)),
        ],
        compiler_params=pltpu.CompilerParams(collective_id=0, has_side_effects=True, vmem_limit_bytes=62 << 20),
    )(img, og, reduce_weight, expand_weight, excite_down, excite_up, fw, sw, mvec, cvec, db, asp)
    saved, fac, (se, fsum, stat_r, stat_e, vb) = list(fwd[:16]), fwd[16], fwd[17:]

    dp = lax.axis_size("dp")
    YB = 2
    ZB = 4 if dp % 8 == 0 else dp // 2
    saved[14] = saved[14].reshape(M, CH)
    saved[15] = saved[15].reshape(2, 2, YB, ZB, quarter // (YB * ZB), 9 * G)
    slots = 2
    pe, pr = quarter // (YB * ZB), CS // (YB * ZB)
    block_out, images_grad, grouped, rw_grad, ew_grad, down_grad, up_grad, va, vl = pl.pallas_call(
        functools.partial(backward_kernel, dims, (YB, ZB)),
        name="backward",
        out_shape=(
            S((H, W, N, CS), BF16), S((H, W, N, CS), F32), S((4, YB, ZB, 2, pe, 9 * G), BF16),
            S((CS, M), F32), S((quarter, 2 * CH), F32), S((CS, M), F32), S((M, CS), F32),
            S((2, 8, M), F32), S((2, 8, M), F32),
        ),
        in_specs=[anyspec] * 18 + [vm] * 7,
        out_specs=[anyspec] * 3 + [vm] * 6,
        scratch_shapes=[
            V((3, W, NI, CH), F32), V((H, W, NI, MH), F32), V((H, W, NI, CH), BF16), V((H, W, NI, CH), BF16),
            V((H, W, NI, M), BF16), V((CH, M), BF16), V((M, CH), BF16),
            V((4, W, NI, MH), F32), V((4, W, NI, MH), F32), V((4, W, NI, MH), F32),
            V((H + 2, W + 2, NI, MH), BF16), V((H + 2, W + 2, NI, MH), BF16), V((9 * G, MH), BF16), V((9 * G, MH), BF16),
            V((CH, M), BF16), V((2, pe, 9 * G), BF16), V((quarter, 2 * CH), BF16),
            V((H * W * NI, 9 * G), BF16), V((H, W, NI, MH), BF16), V((H, W, NI, MH), BF16),
            V((H + 2, W + 2, NI, MH), BF16), V((H + 2, W + 2, NI, MH), BF16),
            V((slots, W, NI, CH), BF16), V((CH, M), BF16), V((2, MH, 9 * G), BF16), V((8, MH), F32), V((8, CH), F32), V((8, M), F32),
            V((YB, ZB, 2, NI, width), BF16),
            V((2, quarter, CH), BF16), V((2, quarter // 2, CH), BF16), V((2, quarter // 2, CH), BF16),
            V((ZB, 2, pe, CH), BF16), V((ZB, 2, pe, CH), BF16), V((2, pe, CH), BF16), V((2, pe, CH), BF16),
            V((YB, ZB, 2, pe, CH), BF16),
            V((1, CS, M), BF16), V((1, CS // 2, M), BF16), V((1, CS // 2, M), BF16),
            V((ZB, 1, pr, M), BF16), V((ZB, 1, pr, M), BF16), V((YB, ZB, 1, pr, M), BF16),
            V((2, quarter, 9 * G), BF16), V((2, quarter // 2, 9 * G), BF16), V((2, quarter // 2, 9 * G), BF16),
            V((ZB, 2, pe, 9 * G), BF16), V((ZB, 2, pe, 9 * G), BF16), V((2, pe, 9 * G), BF16),
            V((2, 8, M), F32), V((2, 8, M), F32), V((ZB, 8, M), F32),
            V((2, 8, M), F32), V((2, 8, M), F32), V((ZB, 8, M), F32),
            DMA((13,)), DMA((H, 3)), DMA((H, 3)), DMA((H,)), DMA((H,)), DMA((H,)), DMA((H,)),
            DMA((H,)), DMA((H,)), DMA((H,)), DMA((H,)), DMA((H,)), DMA((H,)),
            DMA((8,)), DMA((4, ZB)), DMA((6,)), DMA((4, ZB)), DMA((6,)), DMA((4, ZB)), DMA((4, 3)), DMA((4, ZB)),
            DMA((4,)), DMA((2, ZB)), DMA((16,)), DMA((2,)), pltpu.SemaphoreType.REGULAR,
        ],
        compiler_params=pltpu.CompilerParams(collective_id=1, has_side_effects=True, vmem_limit_bytes=63 << 20),
    )(*saved, fac, expand_weight, se, fsum, stat_r, stat_e, vb, mvec, asp)

    grouped = jnp.transpose(grouped, (3, 5, 0, 1, 2, 4)).reshape(2, 3, 3, G, M).astype(F32)
    outs = [grouped[0], grouped[1], rw_grad, ew_grad, down_grad, up_grad, va, vl]
    parts = YB * ZB
    if dp > parts:
        outs = [v / parts for v in lax.psum(tuple(outs), "dp")]
    first_weight_grad, second_weight_grad, rw_grad, ew_grad, down_grad, up_grad, va, vl = outs
    xi, ci = index // 2, index % 2
    mine = lax.dynamic_slice_in_dim(lax.dynamic_index_in_dim(va, xi, 0, keepdims=False), ci * CS, CS, 1)
    late = vl[0] + vl[1]
    back = lambda v: jnp.transpose(v, (2, 0, 1, 3))
    return (
        back(block_out), back(images_grad), rw_grad, late[2], late[3], first_weight_grad, late[4], late[5],
        second_weight_grad, late[6], late[7], ew_grad, mine[0], mine[1], down_grad, va[0, 4], up_grad, mine[2],
        jnp.sum(va[0, 3] + va[1, 3]).reshape(1),
    )


def solution(mesh):
    rows = P("dp", None, None, "chan")
    placed = (
        rows, P("dp"), P("chan", None), P(), P(), P(), P(), P(), P(), P(), P(), P("chan", None), P("chan"), P("chan"),
        P("chan", None), P(), P(None, "chan"), P("chan"), P(), rows,
    )
    results = (
        rows, rows, P("chan", None), P(), P(), P(), P(), P(), P(), P(), P(), P("chan", None), P("chan"), P("chan"),
        P("chan", None), P(), P(None, "chan"), P("chan"), P(),
    )
    return jax.shard_map(body, mesh=mesh, in_specs=placed, out_specs=results, check_vma=False)
```

```python
import functools
import jax
import jax.numpy as jnp
from jax import lax
from jax.experimental import pallas as pl
from jax.experimental.pallas import tpu as pltpu
from jax.sharding import PartitionSpec as P

INV_BETA = 1.0 / 1.16619037896906
ALPHA_RES = 0.2
GELU_SCALE = 1.7015
STD_EPSILON = 0.0001
ROOT = 0.7978845608028654
CUBIC = 0.044715
MESH = pl.DeviceIdType.MESH
F32 = jnp.float32
BF16 = jnp.bfloat16


def gelu(v):
    return 0.5 * v * (1.0 + jnp.tanh(ROOT * v * (1.0 + CUBIC * v * v)))


def gelu_slope(v):
    square = v * v
    t = jnp.tanh(ROOT * v * (1.0 + CUBIC * square))
    return 0.5 * (1.0 + t) + 0.5 * v * (1.0 - t * t) * ROOT * (1.0 + 3.0 * CUBIC * square)


def split3(x):
    high = x.astype(BF16)
    rest = x - high.astype(F32)
    middle = rest.astype(BF16)
    low = (rest - middle.astype(F32)).astype(BF16)
    return jnp.concatenate([high, middle, low], axis=0)


def dot3(x, w, over):
    rows = x.shape[0]
    y = lax.dot_general(split3(x), w, (((1,), (over,)), ((), ())), preferred_element_type=F32)
    return y[:rows] + y[rows : 2 * rows] + y[2 * rows :]


def dot_nt(x, w):
    return lax.dot_general(x, w, (((1,), (1,)), ((), ())), preferred_element_type=F32)


def dot_tn(x, y):
    return lax.dot_general(x, y, (((0,), (0,)), ((), ())), preferred_element_type=F32)


def place():
    d, c = lax.axis_index("dp"), lax.axis_index("chan")
    xi, ci = c // 2, c % 2
    sib = (d, xi * 2 + (1 - ci))
    xn = (d, (1 - xi) * 2 + ci)
    dg = (d, (1 - xi) * 2 + (1 - ci))
    return d, c, xi, ci, sib, xn, dg


def greet(peers):
    barrier = pltpu.get_barrier_semaphore()
    for peer in peers:
        pl.semaphore_signal(barrier, inc=1, device_id=peer, device_id_type=MESH)
    pl.semaphore_wait(barrier, len(peers))


def remote(src, dst, send, recv, peer):
    return pltpu.make_async_remote_copy(
        src_ref=src, dst_ref=dst, send_sem=send, recv_sem=recv, device_id=peer, device_id_type=MESH
    )


def patches(ref, h, lanes, turned, width):
    shifted = [[ref[h + u, v : v + width, :, lanes] for v in range(3)] for u in range(3)]
    parts = []
    for u in range(3):
        for v in range(3):
            if u == v:
                parts.append(shifted[u][v])
            else:
                parts.append(jnp.where(turned, shifted[v][u], shifted[u][v]))
    whole = jnp.concatenate(parts, axis=-1)
    return whole.reshape(whole.shape[0] * whole.shape[1], whole.shape[2])


def conv_row(ref, h, kernel_ref, turned, width, taps):
    groups = kernel_ref.shape[1] // taps
    outs = []
    for g in range(groups):
        outs.append(
            jnp.dot(
                patches(ref, h, slice(g * taps, (g + 1) * taps), turned, width),
                kernel_ref[:, g * taps : (g + 1) * taps],
                preferred_element_type=F32,
            )
        )
    whole = jnp.concatenate(outs, axis=-1)
    return whole.reshape(width, -1, whole.shape[-1])


class Group:
    def __init__(self, shape):
        YB, ZB = shape
        d, c, xi, ci, sib, xn, dg = place()
        self.zb, self.ci, self.xi, self.sib, self.xn = ZB, ci, xi, sib, xn
        self.yb, self.zz = d % YB, (d // YB) % ZB
        first = (d // (YB * ZB)) * (YB * ZB)
        self.yp = (first + self.zz * YB + (1 - self.yb), c)

        def zpeer(k):
            to = lax.rem(self.zz + k, ZB)
            return to, (first + to * YB + self.yb, c)

        self.zpeer = zpeer
        self.zpeers = [zpeer(k)[1] for k in range(1, ZB)]
        self.others = []
        for k in range(ZB):
            to, same = zpeer(k)
            across = (first + to * YB + (1 - self.yb), c)
            if k:
                self.others.append((self.yb, to, same))
            self.others.append((1 - self.yb, to, across))


def forward_kernel(
    dims, group,
    img, og, rw, ew, dn, up, fw, sw, v_rg, v_rb, v_fg, v_fb, v_sg, v_sb, v_eg, v_eb, v_ub, v_db, v_skip, v_asp,
    o_preE, o_og, o_img, o_as2, o_kr, o_ke, o_preR, o_preF, o_preS, o_PR, o_PF, o_kt1, o_kt2,
    o_kraw, o_ewb, o_fac, o_se, o_sum, o_str, o_ste, o_vb, o_mvec, o_asp,
    imgb, ogb, kraw, ewb, dnb, upb, fraw, sraw, st, kr, ke, k1, k2, kt1, kt2, fac,
    preR, s1, r1, PR, PF, preF, preS, as2, preE, acc, px, hx, cvec, aspv,
    loc_img, ss_img, rs_img, loc, ss, rs, ss_st, rs_st, ss1, rs1, ss2, rs2, sx, rx, outs, q_sem, q_zsem, e_out,
):
    H, W, NI, CS, CH, MH, M, G = dims
    d, c, xi, ci, sib, xn, dg = place()
    at = Group(group)
    greet([sib, xn, dg, at.yp] + at.zpeers)
    mine = pl.ds(pl.multiple_of(ci * NI, NI), NI)
    theirs = pl.ds(pl.multiple_of((1 - ci) * NI, NI), NI)
    clan = pl.ds(pl.multiple_of(ci * CS, CS), CS)
    mlan = pl.ds(pl.multiple_of(xi * MH, MH), MH)
    olan = pl.ds(pl.multiple_of((1 - xi) * MH, MH), MH)
    hlan = pl.ds(pl.multiple_of(xi * CH, CH), CH)
    xlan = pl.ds(pl.multiple_of((1 - xi) * CH, CH), CH)
    yb, zz = at.yb, at.zz
    qx = (1 - xi) * 2 + ci

    def img_send(h):
        return remote(img.at[h, :, theirs, :], imgb.at[h, :, :, clan], ss_img.at[h], rs_img.at[h], sib)

    def img_local(h):
        return pltpu.make_async_copy(img.at[h, :, mine, :], imgb.at[h, :, :, clan], loc_img.at[h])

    locals_ = [
        pltpu.make_async_copy(rw, kraw.at[clan, :], loc.at[0]),
        pltpu.make_async_copy(ew.at[:, :, :, hlan], ewb.at[c], loc.at[1]),
        pltpu.make_async_copy(dn, dnb.at[clan, :], loc.at[2]),
        pltpu.make_async_copy(up, upb.at[:, clan], loc.at[3]),
        pltpu.make_async_copy(fw.at[:, mlan], fraw, loc.at[4]),
        pltpu.make_async_copy(sw.at[:, mlan], sraw, loc.at[5]),
        pltpu.make_async_copy(cvec, o_vb.at[:, clan], loc.at[6]),
        pltpu.make_async_copy(og.at[:, :, mine, :], ogb.at[:, :, :, clan], loc.at[7]),
    ]
    sends = [
        remote(rw, kraw.at[clan, :], ss.at[0], rs.at[0], sib),
        remote(ew.at[:, :, :, hlan], ewb.at[c], ss.at[1], rs.at[1], sib),
        remote(dn, dnb.at[clan, :], ss.at[2], rs.at[2], sib),
        remote(up, upb.at[:, clan], ss.at[3], rs.at[3], sib),
        remote(cvec, o_vb.at[:, clan], ss.at[4], rs.at[4], sib),
        remote(og.at[:, :, theirs, :], ogb.at[:, :, :, clan], ss.at[5], rs.at[5], sib),
        remote(ew.at[yb, zz, :, xlan], ewb.at[c, yb, zz], ss.at[6], rs.at[6], xn),
    ]
    locals_[0].start()
    sends[0].start()

    def start_img(h, carry):
        img_local(h).start()
        img_send(h).start()
        return carry

    lax.fori_loop(0, H, start_img, 0)

    def lane_row(ref, first, count):
        return jnp.concatenate([ref[pl.ds(first + k, 1), :] for k in range(count)], axis=-1)

    per_m, per_c = MH // G, CS // G
    half_rows = [lane_row(v, xi * per_m, per_m) for v in (v_rg, v_rb, v_fg, v_fb, v_sg, v_sb)]
    o_mvec[...] = jnp.concatenate(half_rows + [jnp.zeros((2, MH), F32)], axis=0)
    own_rows = [lane_row(v, 0, per_c) for v in (v_eg, v_eb, v_ub)]
    own_rows.append(jnp.broadcast_to(ALPHA_RES * v_skip[...], (1, CS)))
    cvec[...] = jnp.concatenate(own_rows + [jnp.zeros((4, CS), F32)], axis=0)
    down_bias = lane_row(v_db, 0, M // G)
    turn = jnp.concatenate([v_asp[...].astype(F32), jnp.zeros((1, G - v_asp.shape[1]), F32)], axis=-1)
    aspv[...] = jnp.broadcast_to(turn, (G, G)).T
    asp = aspv[mine, :]
    o_asp[...] = asp
    for k in (4, 5, 1, 6, 2, 3, 7):
        locals_[k].start()

    locals_[0].wait()
    own = kraw[clan, :].astype(F32)
    middle = jnp.mean(own, axis=0, keepdims=True)
    away = own - middle
    st[c] = jnp.concatenate(
        [middle, jnp.sum(away * away, axis=0, keepdims=True), jnp.zeros((6, M), F32)], axis=0
    )
    stats = [remote(st.at[c], st.at[c], ss_st.at[k], rs_st.at[c], peer) for k, peer in enumerate((sib, xn, dg))]
    for s in stats:
        s.start()
    for k in (6, 1, 4, 2, 3, 5):
        sends[k].start()

    edge_w = jnp.zeros((W + 2, NI, MH), BF16)
    for ref in (PR, PF):
        ref[0] = edge_w
        ref[H + 1] = edge_w
        for h in range(1, H + 1):
            ref[h, 0] = edge_w[0]
            ref[h, W + 1] = edge_w[0]
    acc[...] = jnp.zeros_like(acc)

    def stat_of(q):
        return remote(st.at[q], st.at[q], ss_st.at[0], rs_st.at[q], sib)

    for k in (1, 2, 3):
        stat_of(lax.rem(c + k, 4)).wait_recv()
    count = CS
    mean = (st[0, 0:1] + st[1, 0:1] + st[2, 0:1] + st[3, 0:1]) * 0.25
    spread = jnp.zeros_like(mean)
    for q in range(4):
        gap = st[q, 0:1] - mean
        spread = spread + st[q, 1:2] + count * gap * gap
    rate = lax.rsqrt(spread + STD_EPSILON)
    o_str[...] = jnp.concatenate([mean, rate, jnp.zeros((6, M), F32)], axis=0)
    sends[0].wait_recv()

    def kr_block(j, carry):
        rows = pl.ds(pl.multiple_of(j * 128, 128), 128)
        kr[rows, :] = ((kraw[rows, :].astype(F32) - mean) * rate).astype(BF16)
        return carry

    lax.fori_loop(0, CH // 128, kr_block, 0)

    def s1_copy(h):
        return remote(s1.at[h], r1.at[h], ss1.at[h], rs1.at[h], xn)

    def reduce_row(h, carry):
        img_local(h).wait()
        img_send(h).wait_recv()
        scaled = (imgb[h].astype(F32) * INV_BETA).astype(BF16).reshape(W * NI, CH)
        s1[h] = (
            jnp.dot(scaled, kr[:, olan], preferred_element_type=F32).astype(BF16).reshape(W, NI, MH)
        )
        s1_copy(h).start()
        preR[h] = jnp.dot(scaled, kr[:, mlan], preferred_element_type=F32).reshape(W, NI, MH)
        return carry

    lax.fori_loop(0, H, reduce_row, 0)

    def q_slot(z):
        return ewb.at[qx, yb, z]

    def q_copy(k):
        return remote(q_slot(zz), q_slot(zz), q_zsem.at[0, k], q_zsem.at[1, zz], at.zpeer(k)[1])

    def q_y(y):
        return remote(ewb.at[qx, y], ewb.at[qx, y], q_sem.at[0], q_sem.at[1], at.yp)

    def q_core(q):
        return remote(ewb.at[q], ewb.at[q], q_sem.at[2], q_sem.at[3], sib)

    remote(q_slot(zz), q_slot(zz), ss.at[6], rs.at[6], xn).wait_recv()
    for k in range(1, at.zb):
        q_copy(k).start()

    for k, raw, kern, trans in ((4, fraw, k1, kt1), (5, sraw, k2, kt2)):
        locals_[k].wait()
        for g in range(MH // G):
            lanes = slice(g * G, (g + 1) * G)
            w = raw[:, lanes].astype(F32)
            w = w - jnp.mean(w, axis=0, keepdims=True)
            w = w * lax.rsqrt(jnp.sum(w * w, axis=0, keepdims=True) + STD_EPSILON)
            kern[:, lanes] = w.astype(BF16)
            for tap in range(9):
                block = kern[(8 - tap) * G : (9 - tap) * G, lanes].astype(F32)
                trans[tap * G : (tap + 1) * G, lanes] = block.T.astype(BF16)

    for k in range(1, at.zb):
        to, peer = at.zpeer(k)
        remote(q_slot(to), q_slot(to), q_zsem.at[0, k], q_zsem.at[1, to], peer).wait_recv()
    q_y(yb).start()

    def expand_kernel():
        locals_[1].wait()
        sends[1].wait_recv()
        q_core((1 - xi) * 2 + (1 - ci)).wait_recv()
        e_stat = []
        for j in range(CH // G):
            lanes = slice(j * G, (j + 1) * G)
            blocks = [ewb[q, :, :, :, lanes].astype(F32).reshape(M // 4, G) for q in range(4)]
            total = sum(jnp.sum(b, axis=0, keepdims=True) for b in blocks)
            e_mean = total / M
            blocks = [b - e_mean for b in blocks]
            squares = sum(jnp.sum(b * b, axis=0, keepdims=True) for b in blocks)
            e_rate = lax.rsqrt(squares + STD_EPSILON)
            for q in range(4):
                ke[q * (M // 4) : (q + 1) * (M // 4), lanes] = (blocks[q] * e_rate).astype(BF16)
            e_stat.append(jnp.concatenate([e_mean, e_rate, jnp.zeros((6, G), F32)], axis=0))
        o_ste[xi] = jnp.concatenate(e_stat, axis=-1)
        ste_copy.start()

    ste_copy = remote(o_ste.at[xi], o_ste.at[xi], sx.at[2], rx.at[2], xn)
    turned = jnp.broadcast_to((asp > 0.5)[None], (W, NI, G))
    mvec = o_mvec
    reduce_gain, reduce_bias = mvec[0:1, :], mvec[1:2, :]
    first_gain, first_bias = mvec[2:3, :], mvec[3:4, :]
    second_gain, second_bias = mvec[4:5, :], mvec[5:6, :]

    locals_[7].wait()
    sends[5].wait_recv()

    def s2_copy(h):
        return remote(as2.at[h, :, :, mlan], as2.at[h, :, :, mlan], ss2.at[h], rs2.at[h], xn)

    def s2_arrival(h):
        return remote(as2.at[h, :, :, olan], as2.at[h, :, :, olan], ss2.at[h], rs2.at[h], xn)

    pairs = (
        (ogb, o_og), (imgb, o_img), (kr, o_kr), (kt1, o_kt1), (kt2, o_kt2), (kraw, o_kraw), (preR, o_preR),
        (preF, o_preF), (preS, o_preS), (PR, o_PR), (PF, o_PF), (as2, o_as2), (ke, o_ke), (ewb, o_ewb),
    )
    saves = [pltpu.make_async_copy(a, b, outs.at[k]) for k, (a, b) in enumerate(pairs)]

    def wave(t, carry):
        @pl.when(t < H)
        def _():
            s1_copy(t).wait_recv()
            pre = preR[t] + r1[t].astype(F32)
            preR[t] = pre
            PR[t + 1, 1 : W + 1] = (GELU_SCALE * gelu(pre * reduce_gain + reduce_bias)).astype(BF16)

        @pl.when((t >= 1) & (t <= H))
        def _():
            pre = conv_row(PR, t - 1, k1, turned, W, G)
            preF[t - 1] = pre
            PF[t, 1 : W + 1] = (GELU_SCALE * gelu(pre * first_gain + first_bias)).astype(BF16)

        @pl.when((t >= 2) & (t <= H + 1))
        def _():
            pre = conv_row(PF, t - 2, k2, turned, W, G)
            preS[t - 2] = pre
            as2[t - 2, :, :, mlan] = (GELU_SCALE * gelu(pre * second_gain + second_bias)).astype(BF16)
            s2_copy(t - 2).start()

        @pl.when(t == 1)
        def _():
            q_y(1 - yb).wait_recv()
            q_core(qx).start()

        @pl.when(t == 3)
        def _():
            expand_kernel()

        return carry

    lax.fori_loop(0, H + 2, wave, 0)
    for k in (12, 13, 6, 7, 8, 9, 10, 0, 1, 2, 3, 4, 5):
        saves[k].start()

    def expand_row(h, carry):
        s2_arrival(h).wait_recv()
        pre = jnp.dot(as2[h].reshape(W * NI, M), ke[...], preferred_element_type=F32).reshape(W, NI, CH)
        preE[h] = pre
        grad = ogb[h].astype(F32)
        acc[0] += jnp.sum(pre, axis=0)
        acc[1] += jnp.sum(grad, axis=0)
        acc[2] += jnp.sum(grad * pre, axis=0)
        pltpu.make_async_copy(preE.at[h], o_preE.at[h], e_out.at[h]).start()
        return carry

    lax.fori_loop(0, H, expand_row, 0)
    saves[11].start()

    for k in (2, 3, 6):
        locals_[k].wait()
    for k in (2, 3, 4):
        sends[k].wait_recv()
    gain, bias = o_vb[0:1, :], o_vb[1:2, :]
    up_bias, branch_scale = o_vb[2:3, :], o_vb[3:4, :]
    pixels = H * W
    sum_pre, sum_grad, sum_both = acc[0], acc[1], acc[2]
    pooled = gain * (sum_pre * (1.0 / pixels)) + bias
    px[xi] = dot3(pooled, dnb[...], 0)
    p_copy = remote(px.at[xi], px.at[xi], sx.at[0], rx.at[0], xn)
    p_copy.start()
    remote(px.at[1 - xi], px.at[1 - xi], sx.at[0], rx.at[0], xn).wait_recv()
    down = px[0] + px[1] + down_bias
    hidden = gelu(down)
    upper = dot3(hidden, upb[...], 0) + up_bias
    sigma = 1.0 / (1.0 + jnp.exp(-upper))
    gating = 2.0 * sigma
    grad_gating_raw = gain * sum_both + bias * sum_grad
    grad_upper = branch_scale * grad_gating_raw * 2.0 * sigma * (1.0 - sigma)
    hx[xi] = dot3(grad_upper, upb[...], 1)
    h_copy = remote(hx.at[xi], hx.at[xi], sx.at[1], rx.at[1], xn)
    h_copy.start()
    remote(hx.at[1 - xi], hx.at[1 - xi], sx.at[1], rx.at[1], xn).wait_recv()
    grad_down = (hx[0] + hx[1]) * gelu_slope(down)
    grad_pooled = dot3(grad_down, dnb[...], 1)
    scaled_gate = branch_scale * gating
    pool_part = grad_pooled * (1.0 / pixels)
    o_se[0] = scaled_gate
    o_se[1] = pool_part
    for s in range(2):
        shard = slice(s * CS, (s + 1) * CS)
        fac[s] = jnp.concatenate([pooled[:, shard], grad_down, hidden, grad_upper[:, shard]], axis=-1).astype(BF16)
    fac_save = pltpu.make_async_copy(fac, o_fac, outs.at[14])
    fac_save.start()
    gain_grad = jnp.sum(scaled_gate * sum_both + pool_part * sum_pre, axis=0, keepdims=True)
    bias_grad = jnp.sum(scaled_gate * sum_grad + grad_pooled, axis=0, keepdims=True)
    up_bias_grad = jnp.sum(grad_upper, axis=0, keepdims=True)
    skip_row = ALPHA_RES * jnp.sum(gating * grad_gating_raw, axis=0, keepdims=True)
    down_bias_grad = jnp.sum(grad_down, axis=0, keepdims=True)
    o_sum[...] = jnp.concatenate(
        [gain_grad, bias_grad, up_bias_grad, skip_row, down_bias_grad, jnp.zeros((3, CH), F32)], axis=0
    )

    remote(o_ste.at[1 - xi], o_ste.at[1 - xi], sx.at[2], rx.at[2], xn).wait_recv()
    for s in (ste_copy, p_copy, h_copy, q_y(yb), q_core(qx)):
        s.wait_send()
    for k in range(1, at.zb):
        q_copy(k).wait_send()
    for s in sends + stats:
        s.wait_send()

    def drain(h, carry):
        img_send(h).wait_send()
        s1_copy(h).wait_send()
        s2_copy(h).wait_send()
        pltpu.make_async_copy(preE.at[h], o_preE.at[h], e_out.at[h]).wait()
        return carry

    lax.fori_loop(0, H, drain, 0)
    for s in saves:
        s.wait()
    fac_save.wait()


class DeviceSum:
    def __init__(self, at, block, rows, sbuf, ysend, ybuf, zsend, zbuf, sem, zsem):
        self.at, self.block, self.rows = at, block, rows
        self.sbuf, self.ysend, self.ybuf, self.zsend, self.zbuf = sbuf, ysend, ybuf, zsend, zbuf
        self.sem, self.zsem = sem, zsem
        self.count = sbuf.shape[0]
        self.half = rows // 2

    def core_copy(self, b):
        ref, base = self.block(b, 1 - self.at.ci)
        src = ref.at[pl.ds(pl.multiple_of(base, 16), self.rows), :]
        return remote(src, self.sbuf.at[b], self.sem.at[2 + 2 * b], self.sem.at[3 + 2 * b], self.at.sib)

    def y_copy(self):
        return remote(self.ysend, self.ybuf, self.sem.at[0], self.sem.at[1], self.at.yp)

    def z_copy(self, k):
        to, peer = self.at.zpeer(k)
        zz = self.at.zz
        return remote(self.zsend.at[to], self.zbuf.at[zz], self.zsem.at[0, k], self.zsem.at[1, zz], peer)

    def z_arrival(self, k):
        to, peer = self.at.zpeer(k)
        return remote(self.zsend.at[to], self.zbuf.at[to], self.zsem.at[0, k], self.zsem.at[1, to], peer)

    def core_sum(self, b, y):
        ref, base = self.block(b, self.at.ci)
        at = pl.multiple_of(y * self.half, 16)
        mine = ref[pl.ds(pl.multiple_of(base + at, 16), self.half), :]
        return mine.astype(F32) + self.sbuf[b, pl.ds(at, self.half), :].astype(F32)

    def to_core(self):
        for b in range(self.count):
            self.core_copy(b).start()

    def to_y(self):
        for b in range(self.count):
            self.core_copy(b).wait_recv()
        for b in range(self.count):
            self.ysend[b] = self.core_sum(b, 1 - self.at.yb).astype(BF16)
        self.y_copy().start()

    def to_z(self):
        self.y_copy().wait_recv()
        piece = self.half // self.at.zb
        for b in range(self.count):
            total = self.core_sum(b, self.at.yb) + self.ybuf[b].astype(F32)
            for z in range(self.at.zb):
                self.zsend[z, b] = total[z * piece : (z + 1) * piece].astype(BF16)
        for k in range(1, self.at.zb):
            self.z_copy(k).start()

    def totals(self):
        for k in range(1, self.at.zb):
            self.z_arrival(k).wait_recv()
        outs = []
        for b in range(self.count):
            total = self.zsend[self.at.zz, b].astype(F32)
            for k in range(1, self.at.zb):
                total = total + self.zbuf[self.at.zpeer(k)[0], b].astype(F32)
            outs.append(total.astype(BF16))
        return outs

    def finish_cores(self):
        for b in range(self.count):
            self.core_copy(b).wait_send()

    def finish(self):
        self.y_copy().wait_send()
        for k in range(1, self.at.zb):
            self.z_copy(k).wait_send()


class Spread:
    def __init__(self, at, piece, full, sem, zsem, lanes=None):
        self.at, self.piece, self.full, self.sem, self.zsem, self.lanes = at, piece, full, sem, zsem, lanes

    def slot(self, y, z=None):
        if self.lanes is None:
            return self.full.at[y] if z is None else self.full.at[y, z]
        return self.full.at[y, :, :, self.lanes] if z is None else self.full.at[y, z, :, self.lanes]

    def keep(self):
        return pltpu.make_async_copy(self.piece, self.slot(self.at.yb, self.at.zz), self.sem.at[2])

    def z_copy(self, k):
        own = self.slot(self.at.yb, self.at.zz)
        return remote(self.piece, own, self.zsem.at[0, k], self.zsem.at[1, self.at.zz], self.at.zpeer(k)[1])

    def y_copy(self):
        own = self.slot(self.at.yb)
        return remote(own, own, self.sem.at[0], self.sem.at[1], self.at.yp)

    def to_z(self):
        self.keep().start()
        for k in range(1, self.at.zb):
            self.z_copy(k).start()

    def to_y(self):
        self.keep().wait()
        for k in range(1, self.at.zb):
            to, peer = self.at.zpeer(k)
            slot = self.slot(self.at.yb, to)
            remote(slot, slot, self.zsem.at[0, k], self.zsem.at[1, to], peer).wait_recv()
        self.y_copy().start()

    def arrive(self):
        slot = self.slot(1 - self.at.yb)
        remote(slot, slot, self.sem.at[0], self.sem.at[1], self.at.yp).wait_recv()

    def finish(self):
        for k in range(1, self.at.zb):
            self.z_copy(k).wait_send()
        self.y_copy().wait_send()


class SpreadYZ(Spread):
    def y_copy(self):
        own = self.slot(self.at.yb, self.at.zz)
        return remote(self.piece, own, self.sem.at[0], self.sem.at[1], self.at.yp)

    def z_copy(self, k):
        own = self.full.at[:, self.at.zz]
        return remote(own, own, self.zsem.at[0, k], self.zsem.at[1, self.at.zz], self.at.zpeer(k)[1])

    def to_y(self):
        self.keep().start()
        self.y_copy().start()

    def to_z(self):
        self.keep().wait()
        slot = self.slot(1 - self.at.yb, self.at.zz)
        remote(slot, slot, self.sem.at[0], self.sem.at[1], self.at.yp).wait_recv()
        for k in range(1, self.at.zb):
            self.z_copy(k).start()

    def arrive(self):
        for k in range(1, self.at.zb):
            to, peer = self.at.zpeer(k)
            slot = self.full.at[:, to]
            remote(slot, slot, self.zsem.at[0, k], self.zsem.at[1, to], peer).wait_recv()


class DirectSum:
    def __init__(self, at, block, rows, sbuf, dsend, dbuf, fin, full, lanes, sem, send_sem, recv_sem):
        self.at, self.block, self.rows = at, block, rows
        self.sbuf, self.dsend, self.dbuf, self.fin, self.full, self.lanes = sbuf, dsend, dbuf, fin, full, lanes
        self.sem, self.send_sem, self.recv_sem = sem, send_sem, recv_sem

    def core_copy(self):
        ref, base = self.block(1 - self.at.ci)
        src = ref.at[pl.ds(pl.multiple_of(base, 16), self.rows), :]
        return remote(src, self.sbuf, self.sem.at[0], self.sem.at[1], self.at.sib)

    def slot(self, y, z):
        return self.full.at[y, z, :, self.lanes]

    def copy(self, phase, k):
        y, z, peer = self.at.others[k]
        yb, zz = self.at.yb, self.at.zz
        if phase == 0:
            src, dst = self.dsend.at[y, z], self.dbuf.at[yb, zz]
        else:
            src, dst = self.fin, self.slot(yb, zz)
        return remote(src, dst, self.send_sem.at[phase, k], self.recv_sem.at[phase, yb, zz], peer)

    def arrival(self, phase, k):
        y, z, peer = self.at.others[k]
        dst = self.dbuf.at[y, z] if phase == 0 else self.slot(y, z)
        return remote(dst, dst, self.send_sem.at[phase, k], self.recv_sem.at[phase, y, z], peer)

    def to_core(self):
        self.core_copy().start()

    def to_owners(self):
        self.core_copy().wait_recv()
        ref, base = self.block(self.at.ci)
        ys, zs, piece = self.dsend.shape[0], self.dsend.shape[1], self.dsend.shape[2]
        half = self.rows // ys
        for y in range(ys):
            mine = ref[pl.ds(pl.multiple_of(base + y * half, 16), half), :]
            total = mine.astype(F32) + self.sbuf[y * half : (y + 1) * half, :].astype(F32)
            for z in range(zs):
                self.dsend[y, z] = total[z * piece : (z + 1) * piece].astype(BF16)
        for k in range(len(self.at.others)):
            self.copy(0, k).start()

    def keep(self):
        return pltpu.make_async_copy(self.fin, self.slot(self.at.yb, self.at.zz), self.sem.at[2])

    def to_all(self):
        total = self.dsend[self.at.yb, self.at.zz].astype(F32)
        for k, (y, z, _) in enumerate(self.at.others):
            self.arrival(0, k).wait_recv()
            total = total + self.dbuf[y, z].astype(F32)
        self.fin[...] = total.astype(BF16)
        self.keep().start()
        for k in range(len(self.at.others)):
            self.copy(1, k).start()

    def arrive(self):
        for k in range(len(self.at.others)):
            self.arrival(1, k).wait_recv()
        self.keep().wait()

    def finish(self):
        self.core_copy().wait_send()
        for phase in range(2):
            for k in range(len(self.at.others)):
                self.copy(phase, k).wait_send()


class VectorSum:
    def __init__(self, at, vs, vy, vz, vx, sem, zsem):
        self.at = at
        self.vs, self.vy, self.vz, self.vx = vs, vy, vz, vx
        self.sem, self.zsem = sem, zsem

    def pair(self, ref, slot, k, peer):
        return remote(ref.at[slot], ref.at[slot], self.sem.at[2 * k], self.sem.at[2 * k + 1], peer)

    def z_pair(self, slot, k, peer):
        return remote(self.vz.at[slot], self.vz.at[slot], self.zsem.at[0, k], self.zsem.at[1, slot], peer)

    def to_core(self, value):
        self.vs[self.at.ci] = value
        self.pair(self.vs, self.at.ci, 0, self.at.sib).start()

    def to_y(self):
        self.pair(self.vs, 1 - self.at.ci, 0, self.at.sib).wait_recv()
        self.vy[self.at.yb] = self.vs[0] + self.vs[1]
        self.pair(self.vy, self.at.yb, 1, self.at.yp).start()

    def to_z(self):
        self.pair(self.vy, 1 - self.at.yb, 1, self.at.yp).wait_recv()
        self.vz[self.at.zz] = self.vy[0] + self.vy[1]
        for k in range(1, self.at.zb):
            self.z_pair(self.at.zz, k, self.at.zpeer(k)[1]).start()

    def to_x(self):
        for k in range(1, self.at.zb):
            to, peer = self.at.zpeer(k)
            self.z_pair(to, k, peer).wait_recv()
        total = self.vz[0]
        for z in range(1, self.at.zb):
            total = total + self.vz[z]
        self.vx[self.at.xi] = total
        self.pair(self.vx, self.at.xi, 2, self.at.xn).start()

    def arrive(self):
        self.pair(self.vx, 1 - self.at.xi, 2, self.at.xn).wait_recv()

    def finish(self):
        self.pair(self.vs, self.at.ci, 0, self.at.sib).wait_send()
        self.pair(self.vy, self.at.yb, 1, self.at.yp).wait_send()
        for k in range(1, self.at.zb):
            self.z_pair(self.at.zz, k, self.at.zpeer(k)[1]).wait_send()
        self.pair(self.vx, self.at.xi, 2, self.at.xn).wait_send()


def backward_kernel(
    dims, group,
    i_preE, i_og, i_img, i_as2, i_kr, i_ke, i_preR, i_preF, i_preS, i_PR, i_PF, i_kt1, i_kt2,
    i_kraw, i_ewb, i_fac, se, fsum, str_, ste, vb, mvec, asp,
    o_block, o_gs, o_G, o_Ge, o_Gr, o_dd, o_du, va, vl, o_rs, o_es,
    preE, gas, ogb, imgb, as2, kr, ke, preR, preF, preS, PR, PF, kt1, kt2, raw,
    wide, s3, r3, GS, GF, bst, gst, Dx, Da, Dt, bsum, estat, rstat, FB,
    e_s, e_ys, e_yb, e_zs, e_zb, e_x, e_fin,
    ra_s, ra_ys, ra_yb, ra_zs, ra_zb, ra_fin, rb_s, rb_send, rb_buf, rb_fin,
    d_s, d_ys, d_yb, d_zs, d_zb, d_fin,
    va_s, va_y, va_z, vl_s, vl_y, vl_z,
    ld, ldr, ldp, ss3, rs3, ss4, rs4, b_loc, b_ss, b_rs, g_loc, g_ss, g_rs,
    e_sem, e_zsem, es_sem, es_zsem, ra_sem, ra_zsem, ras_sem, ras_zsem, rb_sem, rb_ss, rb_rs,
    d_sem, d_zsem, ds_sem, ds_zsem, dc_sem, va_sem, va_zsem, vl_sem, vl_zsem, f_sem, f_zsem, x_sem, credit,
):
    H, W, NI, CS, CH, MH, M, G = dims
    d, c, xi, ci, sib, xn, dg = place()
    at = Group(group)
    yb, zz = at.yb, at.zz
    NG = MH // G
    rows_all = H * W * NI
    RW = W * NI
    pairs = (
        (i_kr, kr), (i_ke, ke), (i_kt1, kt1), (i_kt2, kt2), (i_PR, PR), (i_PF, PF), (i_as2, as2),
        (i_kraw, raw), (i_ewb, raw), (i_fac.at[ci], FB.at[yb, zz, ci]),
    )
    loads = [pltpu.make_async_copy(a, b, ld.at[k]) for k, (a, b) in enumerate(pairs)]
    slots, ring = bst.shape[0], preE.shape[0]
    gpe = pl.ds(0, CH)

    def row_load(h, k):
        src, dst = ((i_preE, preE.at[lax.rem(h, ring)]), (i_og, ogb.at[h]), (i_img, imgb.at[h]))[k]
        return pltpu.make_async_copy(src.at[h], dst, ldr.at[h, k])

    loads[1].start()
    for h in range(ring):
        for k in range(3):
            row_load(h, k).start()
    loads[9].start()

    def pre_load(k, h):
        src, dst = ((i_preS, preS), (i_preF, preF), (i_preR, preR))[k]
        return pltpu.make_async_copy(src.at[h], dst.at[lax.rem(h, 4)], ldp.at[h, k])

    greet([sib, xn] + [peer for _, _, peer in at.others])
    fac_core = remote(i_fac.at[1 - ci], FB.at[yb, zz, ci], f_sem.at[2], f_sem.at[3], sib)
    fac_core.start()
    for k in (6, 8, 5, 3, 4, 2, 0):
        loads[k].start()

    mine = pl.ds(pl.multiple_of(ci * NI, NI), NI)
    clan = pl.ds(pl.multiple_of(ci * CS, CS), CS)
    slan = pl.ds(pl.multiple_of((1 - ci) * CS, CS), CS)
    mlan = pl.ds(pl.multiple_of(xi * MH, MH), MH)
    olan = pl.ds(pl.multiple_of((1 - xi) * MH, MH), MH)
    hlan = pl.ds(pl.multiple_of(xi * CH, CH), CH)
    edge_w = jnp.zeros((W + 2, NI, MH), BF16)
    for ref in (GS, GF):
        ref[0] = edge_w
        ref[H + 1] = edge_w
        for h in range(1, H + 1):
            ref[h, 0] = edge_w[0]
            ref[h, W + 1] = edge_w[0]
    bsum[...] = jnp.zeros_like(bsum)
    estat[...] = jnp.zeros_like(estat)
    rstat[...] = jnp.zeros_like(rstat)

    gain, bias = vb[0:1, :], vb[1:2, :]
    scaled_gate, pool_part = se[0], se[1]

    def row_out(stage, out, loc, ss, rs):
        def local(h):
            return pltpu.make_async_copy(stage.at[lax.rem(h, slots), :, :, clan], out.at[h, :, mine, :], loc.at[h])

        def send(h):
            return remote(
                stage.at[lax.rem(h, slots), :, :, slan], out.at[h, :, mine, :], ss.at[h], rs.at[h], sib
            )

        return local, send

    block_local, block_send = row_out(bst, o_block, b_loc, b_ss, b_rs)
    gs_local, gs_send = row_out(gst, o_gs, g_loc, g_ss, g_rs)

    def s3_copy(h):
        return remote(s3.at[h], r3.at[h], ss3.at[h], rs3.at[h], xn)

    def row_at(h):
        return pl.ds(pl.multiple_of(h * RW, RW), RW)

    loads[1].wait()

    def expand_row(h, carry):
        for k in range(3):
            row_load(h, k).wait()

        @pl.when(h >= slots)
        def _():
            block_local(h - slots).wait()
            block_send(h - slots).wait_send()

        pre = preE[lax.rem(h, ring)]
        grad = ogb[h].astype(F32) * scaled_gate + pool_part
        piece = (grad * gain).astype(BF16).reshape(RW, CH)
        s3[h] = dot_nt(piece, ke[olan, :]).astype(BF16).reshape(W, NI, MH)
        s3_copy(h).start()
        wide[row_at(h), gpe] = piece
        gas[h] = dot_nt(piece, ke[mlan, :]).reshape(W, NI, MH)
        out = pre * gain + bias
        bst[lax.rem(h, slots)] = (imgb[h].astype(F32) + out * scaled_gate).astype(BF16)
        block_local(h).start()
        block_send(h).start()

        @pl.when(h + ring < H)
        def _():
            for k in range(3):
                row_load(h + ring, k).start()

        return carry

    lax.fori_loop(0, H, expand_row, 0)
    pre_load(0, 0).start()
    pre_load(0, 1).start()
    pre_load(1, 0).start()

    loads[9].wait()
    remote(i_fac.at[1 - ci], FB.at[yb, zz, 1 - ci], f_sem.at[2], f_sem.at[3], sib).wait_recv()

    def f_copy(k):
        own = FB.at[yb, zz]
        return remote(own, own, f_zsem.at[0, k], f_zsem.at[1, zz], at.zpeer(k)[1])

    def f_y():
        return remote(FB.at[yb], FB.at[yb], f_sem.at[0], f_sem.at[1], at.yp)

    for k in range(1, at.zb):
        f_copy(k).start()

    loads[6].wait()
    quarter = e_s.shape[1]
    step = 256
    e_mean = ste[xi, 0:1, :]

    def expand_kernel_grad(j, carry):
        lanes = pl.ds(pl.multiple_of(j * step, step), step)
        left = as2[:, :, :, lanes].reshape(rows_all, step)
        Dx[lanes, :] = dot_tn(left, wide[:, gpe]).astype(BF16)
        return carry

    lax.fori_loop(0, M // step, expand_kernel_grad, 0)
    pl.semaphore_signal(credit, inc=1, device_id=xn, device_id_type=MESH)
    gpr = as2

    sum_e = DeviceSum(
        at, lambda b, half: (Dx, b * MH + half * quarter), quarter, e_s, e_ys, e_yb, e_zs, e_zb, e_sem, e_zsem
    )
    sum_e.to_core()
    spread_e = SpreadYZ(at, e_fin, o_Ge, es_sem, es_zsem)

    def e_cross(x):
        lanes = pl.ds(pl.multiple_of(x * CH, CH), CH)
        return remote(e_x.at[1 - x], e_fin.at[:, lanes], x_sem.at[0], x_sem.at[1], xn)

    loads[8].wait()
    for q in range(4):
        grads = Dx[q * quarter : (q + 1) * quarter, :].astype(F32)
        away = raw[q * quarter : (q + 1) * quarter, :].astype(F32) - e_mean
        estat[0:1, :] += jnp.sum(grads, axis=0, keepdims=True)
        estat[1:2, :] += jnp.sum(grads * away, axis=0, keepdims=True)
    loads[7].start()
    sum_a = VectorSum(at, va_s, va_y, va_z, va, va_sem, va_zsem)
    sum_a.to_core(jnp.concatenate([fsum[0:5, :], estat[0:2, :], jnp.zeros((1, CH), F32)], axis=0))

    for k in (5, 3, 4, 2, 0):
        loads[k].wait()
    turned = jnp.broadcast_to((asp[...] > 0.5)[None], (W, NI, G))
    reduce_gain, reduce_bias = mvec[0:1, :], mvec[1:2, :]
    first_gain, first_bias = mvec[2:3, :], mvec[3:4, :]
    second_gain, second_bias = mvec[4:5, :], mvec[5:6, :]

    def s4_copy(h):
        return remote(gpr.at[h, :, :, mlan], gpr.at[h, :, :, mlan], ss4.at[h], rs4.at[h], xn)

    def s4_arrival(h):
        return remote(gpr.at[h, :, :, olan], gpr.at[h, :, :, olan], ss4.at[h], rs4.at[h], xn)

    def tally(row, grad, pre):
        flat = (grad * pre).reshape(RW, MH)
        bsum[row : row + 1, :] += jnp.sum(flat, axis=0, keepdims=True)
        bsum[row + 1 : row + 2, :] += jnp.sum(grad.reshape(RW, MH), axis=0, keepdims=True)

    def image_row(h):
        s4_arrival(h).wait_recv()

        @pl.when(h >= slots)
        def _():
            gs_local(h - slots).wait()
            gs_send(h - slots).wait_send()

        gst[lax.rem(h, slots)] = dot_nt(gpr[h].reshape(RW, M), kr[...]).astype(BF16).reshape(W, NI, CH)
        gs_local(h).start()
        gs_send(h).start()

    part = H // 2

    def group_term(act, cot, g, low):
        lanes = pl.ds(pl.multiple_of(g * G, G), G)

        def fill(h, carry):
            wide[row_at(h), :] = patches(act, low + h, lanes, turned, W)
            return carry

        lax.fori_loop(0, part, fill, 0)
        right = cot[1 + low : 1 + low + part, 1 : W + 1, :, lanes].reshape(part * RW, G)
        return dot_tn(right, wide[0 : part * RW, :])

    def first_half(b, act, cot, g):
        Da[b, pl.ds(pl.multiple_of(g * G, G), G), :] = group_term(act, cot, g, 0)

    def second_half(b, act, cot, low, high):
        def one(g, carry):
            lanes = pl.ds(pl.multiple_of(g * G, G), G)
            total = Da[b, lanes, :] + group_term(act, cot, g, part)
            for tap in range(9):
                block = total[:, tap * G : (tap + 1) * G]
                Dt[b, tap * G : (tap + 1) * G, lanes] = block.T.astype(BF16)
            return carry

        lax.fori_loop(low, high, one, 0)

    def wave(t, carry):
        @pl.when(t + 2 < H)
        def _():
            pre_load(0, t + 2).start()

        @pl.when(t + 1 < H)
        def _():
            pre_load(1, t + 1).start()

        @pl.when(t < H)
        def _():
            pre_load(2, t).start()

        @pl.when(t < H)
        def _():
            pre_load(0, t).wait()
            s3_copy(t).wait_recv()
            cot = (gas[t] + r3[t].astype(F32)).astype(BF16).astype(F32)
            pre = preS[lax.rem(t, 4)]
            grad = cot * (GELU_SCALE * gelu_slope(pre * second_gain + second_bias))
            tally(4, grad, pre)
            GS[t + 1, 1 : W + 1] = (grad * second_gain).astype(BF16)

        @pl.when((t >= 1) & (t <= H))
        def _():
            pre_load(1, t - 1).wait()
            cot = conv_row(GS, t - 1, kt2, turned, W, G)
            pre = preF[lax.rem(t - 1, 4)]
            grad = cot * (GELU_SCALE * gelu_slope(pre * first_gain + first_bias))
            tally(2, grad, pre)
            GF[t, 1 : W + 1] = (grad * first_gain).astype(BF16)

        @pl.when(t == 2)
        def _():
            pl.semaphore_wait(credit, 1)

        @pl.when((t >= 2) & (t <= H + 1))
        def _():
            pre_load(2, t - 2).wait()
            cot = conv_row(GF, t - 2, kt1, turned, W, G)
            pre = preR[lax.rem(t - 2, 4)]
            grad = cot * (GELU_SCALE * gelu_slope(pre * reduce_gain + reduce_bias))
            tally(0, grad, pre)
            gpr[t - 2, :, :, mlan] = (grad * reduce_gain).astype(BF16)
            s4_copy(t - 2).start()

        @pl.when(t == 1)
        def _():
            sum_e.to_y()
            sum_a.to_y()

        @pl.when(t == 2)
        def _():
            for k in range(1, at.zb):
                to, peer = at.zpeer(k)
                slot = FB.at[yb, to]
                remote(slot, slot, f_zsem.at[0, k], f_zsem.at[1, to], peer).wait_recv()
            f_y().start()

        @pl.when(t == 3)
        def _():
            sum_e.to_z()
            sum_a.to_z()

        @pl.when(t == 4)
        def _():
            sum_a.to_x()
            outs = sum_e.totals()
            for b in range(2):
                e_x[b] = outs[b]
            e_fin[:, hlan] = e_x[xi]
            e_cross(xi).start()

        @pl.when(t == H)
        def _():
            e_cross(1 - xi).wait_recv()
            spread_e.to_y()

        @pl.when((t >= 5) & (t < 5 + NG))
        def _():
            first_half(1, PF, GS, t - 5)

        @pl.when((t >= 6) & (t < 6 + NG))
        def _():
            first_half(0, PR, GF, t - 6)

        return carry

    lax.fori_loop(0, H + 2, wave, 0)

    half = 9 * G // 2

    def grouped_jobs(b):
        job = DeviceSum(
            at, lambda _, h: (Dt.at[b], h * half), half, d_s.at[b], d_ys.at[b], d_yb.at[b], d_zs.at[b], d_zb.at[b],
            d_sem.at[b], d_zsem.at[b],
        )
        return job, Spread(at, d_fin.at[b], o_G.at[b, ci], ds_sem.at[b], ds_zsem.at[b], mlan)

    def d_cross(b, y, lanes):
        block = o_G.at[b, ci, y, :, :, lanes]
        return remote(block, block, dc_sem.at[b, y, 0], dc_sem.at[b, y, 1], xn)

    def d_core(b, h, y, lanes, k):
        block = o_G.at[b, h, y, :, :, lanes]
        return remote(block, block, dc_sem.at[b, y, 2 + 2 * k], dc_sem.at[b, y, 3 + 2 * k], sib)

    def reduce_kernel_grad(lanes_m, base):
        r_step = 256
        mean = str_[0:1, lanes_m]

        def one(j, carry):
            lanes = pl.ds(pl.multiple_of(j * r_step, r_step), r_step)
            left = (imgb[:, :, :, lanes].astype(F32) * INV_BETA).astype(BF16).reshape(rows_all, r_step)
            grads = dot_tn(left, gpr[:, :, :, lanes_m].reshape(rows_all, MH))
            rstat[0:1, lanes_m] += jnp.sum(grads, axis=0, keepdims=True)
            rstat[1:2, lanes_m] += jnp.sum(grads * (raw[lanes, lanes_m].astype(F32) - mean), axis=0, keepdims=True)
            Dx[lanes, base : base + MH] = grads.astype(BF16)
            return carry

        lax.fori_loop(0, CH // r_step, one, 0)

    def reduce_jobs(base, lanes, bufs, sem, zsem, fin, s_sem, s_zsem):
        job = DeviceSum(at, lambda b, h: (Dx.at[:, base : base + MH], h * CS), CS, *bufs, sem, zsem)
        return job, Spread(at, fin, o_Gr, s_sem, s_zsem, lanes)

    sum_1, spread_1 = grouped_jobs(0)
    sum_2, spread_2 = grouped_jobs(1)
    sum_ra, spread_ra = reduce_jobs(
        0, mlan, (ra_s, ra_ys, ra_yb, ra_zs, ra_zb), ra_sem, ra_zsem, ra_fin, ras_sem, ras_zsem
    )
    sum_rb = DirectSum(
        at, lambda h: (Dx.at[:, MH : 2 * MH], h * CS), CS, rb_s, rb_send, rb_buf, rb_fin, o_Gr, olan, rb_sem, rb_ss, rb_rs
    )
    sum_l = VectorSum(at, vl_s, vl_y, vl_z, vl, vl_sem, vl_zsem)

    rows = iter(range(H))

    def image(count):
        for _ in range(count):
            for h in rows:
                image_row(h)
                break

    spread_e.to_z()
    second_half(1, PF, GS, 0, NG)
    sum_2.to_core()
    second_half(0, PR, GF, 0, 1)
    sum_2.to_y()
    second_half(0, PR, GF, 1, NG)
    sum_1.to_core()
    sum_2.to_z()
    loads[7].wait()
    sum_e.finish_cores()
    reduce_kernel_grad(mlan, 0)
    sum_ra.to_core()
    sum_1.to_y()
    d_fin[1] = sum_2.totals()[0]
    spread_2.to_z()
    image(2)
    sum_ra.to_y()
    sum_1.to_z()
    image(2)
    spread_2.to_y()
    d_core(1, ci, yb, mlan, 0).start()
    d_cross(1, yb, mlan).start()
    image(1)
    d_fin[0] = sum_1.totals()[0]
    spread_1.to_z()
    sum_ra.to_z()
    image(2)
    spread_1.to_y()
    d_core(0, ci, yb, mlan, 0).start()
    d_cross(0, yb, mlan).start()
    spread_2.arrive()
    d_core(1, ci, 1 - yb, mlan, 0).start()
    d_cross(1, 1 - yb, mlan).start()
    image(1)
    ra_fin[...] = sum_ra.totals()[0]
    spread_ra.to_z()
    for h in rows:
        image_row(h)
    reduce_kernel_grad(olan, MH)
    sum_rb.to_core()
    rstat[2:8, mlan] = bsum[0:6, :]
    sum_l.to_core(rstat[...])
    spread_1.arrive()
    d_core(0, ci, 1 - yb, mlan, 0).start()
    d_cross(0, 1 - yb, mlan).start()
    sum_rb.to_owners()
    sum_l.to_y()
    spread_ra.to_y()
    sum_l.to_z()
    sum_rb.to_all()
    sum_l.to_x()
    d_cross(1, yb, olan).wait_recv()
    d_core(1, ci, yb, olan, 1).start()
    remote(FB.at[1 - yb], FB.at[1 - yb], f_sem.at[0], f_sem.at[1], at.yp).wait_recv()
    fac_all = FB[...].reshape(-1, FB.shape[-1])
    o_dd[...] = dot_tn(fac_all[:, 0:CS], fac_all[:, CS : CS + M]).astype(BF16)
    o_du[...] = dot_tn(fac_all[:, CS + M : CS + 2 * M], fac_all[:, CS + 2 * M :]).astype(BF16)
    d_cross(0, yb, olan).wait_recv()
    d_core(0, ci, yb, olan, 1).start()
    d_cross(1, 1 - yb, olan).wait_recv()
    d_core(1, ci, 1 - yb, olan, 1).start()
    d_cross(0, 1 - yb, olan).wait_recv()
    d_core(0, ci, 1 - yb, olan, 1).start()
    spread_e.arrive()
    spread_ra.arrive()
    sum_rb.arrive()
    sum_a.arrive()
    sum_l.arrive()
    late = vl[0] + vl[1]
    o_rs[...] = jnp.concatenate([str_[0:2, :], late[0:1] * (1.0 / (4 * CS)), late[1:2]], axis=0)
    for x in range(2):
        o_es[:, x * CH : (x + 1) * CH] = jnp.concatenate(
            [ste[x, 0:2, :], va[x, 5:6, :] * (1.0 / (4 * quarter)), va[x, 6:7, :]], axis=0
        )
    for b in range(2):
        for y in range(2):
            for k, lanes in ((0, mlan), (1, olan)):
                d_core(b, 1 - ci, y, lanes, k).wait_recv()

    fac_core.wait_send()
    for k in range(1, at.zb):
        f_copy(k).wait_send()
    f_y().wait_send()
    e_cross(xi).wait_send()
    for b in range(2):
        for y in range(2):
            d_cross(b, y, mlan).wait_send()
            d_core(b, ci, y, mlan, 0).wait_send()
            d_core(b, ci, y, olan, 1).wait_send()
    for job in (sum_1, sum_2, sum_ra):
        job.finish_cores()
    for job in (sum_e, spread_e, sum_a, sum_1, sum_2, spread_1, spread_2, sum_ra, spread_ra, sum_rb, sum_l):
        job.finish()

    def drain(h, carry):
        s3_copy(h).wait_send()
        s4_copy(h).wait_send()
        block_send(h).wait_recv()
        gs_send(h).wait_recv()
        return carry

    lax.fori_loop(0, H, drain, 0)
    for h in range(H - slots, H):
        block_local(h).wait()
        block_send(h).wait_send()
        gs_local(h).wait()
        gs_send(h).wait_send()


def finish_kernel(steps, og, gs, g1, g2, fw, sw, gr, rw, rs, ge, ew, es, dd, du,
                  o_ig, o_g1, o_g2, o_rw, o_ew, o_dd, o_du):
    o_ig[...] = og[...].astype(F32) + INV_BETA * gs[...].astype(F32)

    @pl.when(pl.program_id(0) < steps)
    def _():
        for grad, weight, out in ((g1, fw, o_g1), (g2, sw, o_g2)):
            total, away = grad[...].astype(F32), weight[...].astype(F32)
            away = away - jnp.mean(away, axis=0, keepdims=True)
            rate = lax.rsqrt(jnp.sum(away * away, axis=0, keepdims=True) + STD_EPSILON)
            cross = jnp.sum(total * away, axis=0, keepdims=True) * (rate * rate * rate)
            out[...] = rate * (total - jnp.mean(total, axis=0, keepdims=True)) - away * cross
        for grad, weight, rows, out in ((gr, rw, rs, o_rw), (ge, ew, es, o_ew)):
            mean, rate, low, cross = (rows[k : k + 1, :] for k in range(4))
            away = weight[...].astype(F32) - mean
            out[...] = rate * (grad[...].astype(F32) - low) - away * (cross * (rate * rate * rate))
        o_dd[...] = dd[...].astype(F32)
        o_du[...] = du[...].astype(F32)


def body(
    images, aspect, reduce_weight, reduce_gain, reduce_bias, first_weight, first_gain, first_bias,
    second_weight, second_gain, second_bias, expand_weight, expand_gain, expand_bias, excite_down,
    excite_down_bias, excite_up, excite_up_bias, skip_gain, out_grad,
):
    N, H, W, CS = images.shape
    M = reduce_weight.shape[1]
    G = first_weight.shape[2]
    NI, MH, CH = N // 2, M // 2, 2 * CS
    dims = (H, W, NI, CS, CH, MH, M, G)
    quarter = expand_weight.shape[0]
    index = lax.axis_index("chan")
    dp = lax.axis_size("dp")
    YB = 2
    ZB = 4 if dp % 8 == 0 else dp // 2
    group = (YB, ZB)
    pe, pr, pd = quarter // (YB * ZB), CS // (YB * ZB), 9 * G // (2 * YB * ZB)
    img = jnp.transpose(images, (1, 2, 0, 3))
    og = jnp.transpose(out_grad, (1, 2, 0, 3))
    fw = first_weight.reshape(9 * G, M)
    sw = second_weight.reshape(9 * G, M)
    vectors = [reduce_gain, reduce_bias, first_gain, first_bias, second_gain, second_bias, expand_gain, expand_bias,
               excite_up_bias, excite_down_bias]
    vectors = [v.reshape(-1, G) for v in vectors] + [skip_gain.reshape(1, 1), aspect.reshape(1, N)]

    anyspec = pl.BlockSpec(memory_space=pl.ANY)
    vm = pl.BlockSpec(memory_space=pltpu.VMEM)
    S = jax.ShapeDtypeStruct
    V = pltpu.VMEM
    DMA = pltpu.SemaphoreType.DMA
    width = 2 * CS + 2 * M
    big = (
        S((H, W, NI, CH), F32), S((H, W, NI, CH), BF16), S((H, W, NI, CH), BF16), S((H, W, NI, M), BF16),
        S((CH, M), BF16), S((M, CH), BF16), S((H, W, NI, MH), F32), S((H, W, NI, MH), F32), S((H, W, NI, MH), F32),
        S((H + 2, W + 2, NI, MH), BF16), S((H + 2, W + 2, NI, MH), BF16), S((9 * G, MH), BF16), S((9 * G, MH), BF16),
        S((CH, M), BF16), S((4, YB, ZB, pe, CH), BF16), S((2, NI, width), BF16),
    )
    few = (
        S((2, NI, CH), F32), S((8, CH), F32), S((8, M), F32), S((2, 8, CH), F32), S((8, CH), F32), S((8, MH), F32),
        S((NI, G), F32),
    )
    fwd = pl.pallas_call(
        functools.partial(forward_kernel, dims, group),
        name="forward",
        out_shape=big + few,
        in_specs=[anyspec] * 8 + [vm] * 12,
        out_specs=[anyspec] * 16 + [vm] * 7,
        scratch_shapes=[
            V((H, W, NI, CH), BF16), V((H, W, NI, CH), BF16), V((CH, M), BF16), V((4, YB, ZB, pe, CH), BF16),
            V((CH, M), BF16), V((M, CH), BF16), V((9 * G, MH), BF16), V((9 * G, MH), BF16), V((4, 8, M), F32),
            V((CH, M), BF16), V((M, CH), BF16), V((9 * G, MH), BF16), V((9 * G, MH), BF16), V((9 * G, MH), BF16),
            V((9 * G, MH), BF16), V((2, NI, width), BF16),
            V((H, W, NI, MH), F32), V((H, W, NI, MH), BF16), V((H, W, NI, MH), BF16),
            V((H + 2, W + 2, NI, MH), BF16), V((H + 2, W + 2, NI, MH), BF16),
            V((H, W, NI, MH), F32), V((H, W, NI, MH), F32), V((H, W, NI, M), BF16), V((H, W, NI, CH), F32),
            V((3, NI, CH), F32), V((2, NI, M), F32), V((2, NI, M), F32), V((8, CS), F32), V((G, G), F32),
            DMA((H,)), DMA((H,)), DMA((H,)), DMA((8,)), DMA((8,)), DMA((8,)), DMA((3,)), DMA((4,)),
            DMA((H,)), DMA((H,)), DMA((H,)), DMA((H,)), DMA((3,)), DMA((3,)), DMA((16,)), DMA((4,)), DMA((2, ZB)), DMA((H,)),
        ],
        compiler_params=pltpu.CompilerParams(collective_id=0, has_side_effects=True, vmem_limit_bytes=62 << 20),
    )(img, og, reduce_weight, expand_weight.reshape(YB, ZB, pe, 2 * CH), excite_down, excite_up, fw, sw, *vectors)
    saved, fac, (se, fsum, stat_r, stat_e, vb, mvec, asp) = list(fwd[:15]), fwd[15], fwd[16:]
    saved[14] = saved[14].reshape(M, CH)

    slots = 2
    sums_e = [V((2, quarter, CH), BF16)] + [V((2, quarter // 2, CH), BF16)] * 2 + [V((ZB, 2, pe, CH), BF16)] * 2
    sums_r = [V((1, CS, MH), BF16)] + [V((1, CS // 2, MH), BF16)] * 2 + [V((ZB, 1, pr, MH), BF16)] * 2
    half = 9 * G // 2
    sums_d = [V((2, 1, half, MH), BF16)] + [V((2, 1, half // 2, MH), BF16)] * 2 + [V((2, ZB, 1, pd, MH), BF16)] * 2
    sums_v = [V((2, 8, M), F32), V((2, 8, M), F32), V((ZB, 8, M), F32)]
    block_out, gs, grouped, ew_sum, rw_sum, down_sum, up_sum, va, vl, rs, es = pl.pallas_call(
        functools.partial(backward_kernel, dims, group),
        name="backward",
        out_shape=(
            S((H, W, N, CS), BF16), S((H, W, N, CS), BF16), S((2, 2, YB, ZB, pd, M), BF16),
            S((YB, ZB, pe, 2 * CH), BF16), S((YB, ZB, pr, M), BF16), S((CS, M), BF16), S((M, CS), BF16),
            S((2, 8, M), F32), S((2, 8, M), F32), S((4, M), F32), S((4, 2 * CH), F32),
        ),
        in_specs=[anyspec] * 16 + [vm] * 7,
        out_specs=[anyspec] * 5 + [vm] * 6,
        scratch_shapes=[
            V((3, W, NI, CH), F32), V((H, W, NI, MH), F32), V((H, W, NI, CH), BF16), V((H, W, NI, CH), BF16),
            V((H, W, NI, M), BF16), V((CH, M), BF16), V((M, CH), BF16),
            V((4, W, NI, MH), F32), V((4, W, NI, MH), F32), V((4, W, NI, MH), F32),
            V((H + 2, W + 2, NI, MH), BF16), V((H + 2, W + 2, NI, MH), BF16), V((9 * G, MH), BF16), V((9 * G, MH), BF16),
            V((CH, M), BF16),
            V((H * W * NI, 9 * G), BF16), V((H, W, NI, MH), BF16), V((H, W, NI, MH), BF16),
            V((H + 2, W + 2, NI, MH), BF16), V((H + 2, W + 2, NI, MH), BF16),
            V((slots, W, NI, CH), BF16), V((slots, W, NI, CH), BF16), V((CH, M), BF16), V((2, MH, 9 * G), F32),
            V((2, 9 * G, MH), BF16), V((8, MH), F32), V((8, CH), F32), V((8, M), F32), V((YB, ZB, 2, NI, width), BF16),
            *sums_e, V((2, pe, CH), BF16), V((pe, 2 * CH), BF16),
            *sums_r, V((pr, MH), BF16),
            V((CS, MH), BF16), V((YB, ZB, pr, MH), BF16), V((YB, ZB, pr, MH), BF16), V((pr, MH), BF16),
            *sums_d, V((2, pd, MH), BF16),
            *sums_v, *sums_v,
            DMA((10,)), DMA((H, 3)), DMA((H, 3)), DMA((H,)), DMA((H,)), DMA((H,)), DMA((H,)),
            DMA((H,)), DMA((H,)), DMA((H,)), DMA((H,)), DMA((H,)), DMA((H,)),
            DMA((6,)), DMA((2, ZB)), DMA((3,)), DMA((2, ZB)), DMA((4,)), DMA((2, ZB)), DMA((3,)), DMA((2, ZB)),
            DMA((3,)), DMA((2, YB * ZB)), DMA((2, YB, ZB)),
            DMA((2, 4)), DMA((2, 2, ZB)), DMA((2, 3)), DMA((2, 2, ZB)), DMA((2, 2, 6)),
            DMA((6,)), DMA((2, ZB)), DMA((6,)), DMA((2, ZB)), DMA((4,)), DMA((2, ZB)), DMA((6,)),
            pltpu.SemaphoreType.REGULAR,
        ],
        compiler_params=pltpu.CompilerParams(collective_id=1, has_side_effects=True, vmem_limit_bytes=63 << 20),
    )(*saved, fac, se, fsum, stat_r, stat_e, vb, mvec, asp)

    parts = YB * ZB
    grouped = grouped.reshape(2, 9 * G, M)
    ew_sum, rw_sum = ew_sum.reshape(quarter, 2 * CH), rw_sum.reshape(CS, M)
    if dp > parts:
        whole = [v.astype(F32) for v in (grouped, ew_sum, rw_sum, down_sum, up_sum, va, vl)]
        whole = [v / parts for v in lax.psum(tuple(whole), "dp")]
        grouped, ew_sum, rw_sum, down_sum, up_sum = (v.astype(BF16) for v in whole[:5])
        va, vl = whole[5:]
        low = (vl[0] + vl[1])[0:2]
        rs = jnp.concatenate([rs[0:2], low[0:1] * (1.0 / (4 * CS)), low[1:2]], axis=0)
        low = jnp.concatenate([va[0, 5:7], va[1, 5:7]], axis=1)
        es = jnp.concatenate([es[0:2], low[0:1] * (1.0 / (4 * quarter)), low[1:2]], axis=0)
    late = vl[0] + vl[1]

    per = 5 if H % 5 == 0 else 1
    share = 3 * G
    steps = M // share
    spot = lambda h: jnp.minimum(h, steps - 1)
    row = pl.BlockSpec((per, W, N, CS), lambda h: (h, 0, 0, 0))
    lane = lambda rows, lanes: pl.BlockSpec((rows, lanes), lambda h: (0, spot(h)))
    tall = lambda rows, lanes: pl.BlockSpec((rows, lanes), lambda h: (spot(h), 0))
    which = lambda k: pl.BlockSpec((None, 9 * G, share), lambda h: (k, 0, spot(h)))
    wide = 2 * CH // steps
    outs = pl.pallas_call(
        functools.partial(finish_kernel, steps),
        name="finish",
        grid=(H // per,),
        out_shape=(
            S((H, W, N, CS), F32), S((9 * G, M), F32), S((9 * G, M), F32),
            S((CS, M), F32), S((quarter, 2 * CH), F32), S((CS, M), F32), S((M, CS), F32),
        ),
        in_specs=[
            row, row, which(0), which(1), lane(9 * G, share), lane(9 * G, share), lane(CS, share), lane(CS, share), lane(4, share),
            lane(quarter, wide), lane(quarter, wide), lane(4, wide), lane(CS, share), tall(share, CS),
        ],
        out_specs=[
            row, lane(9 * G, share), lane(9 * G, share), lane(CS, share), lane(quarter, wide), lane(CS, share), tall(share, CS),
        ],
        compiler_params=pltpu.CompilerParams(vmem_limit_bytes=60 << 20),
    )(og, gs, grouped, grouped, fw, sw, rw_sum, reduce_weight, rs, ew_sum, expand_weight, es, down_sum, up_sum)
    images_grad, first_grad, second_grad, rw_grad, ew_grad, down_grad, up_grad = outs

    xi, ci = index // 2, index % 2
    mine = lax.dynamic_slice_in_dim(lax.dynamic_index_in_dim(va, xi, 0, keepdims=False), ci * CS, CS, 1)
    back = lambda v: jnp.transpose(v, (2, 0, 1, 3))
    return (
        back(block_out), back(images_grad), rw_grad, late[2], late[3], first_grad.reshape(3, 3, G, M), late[4], late[5],
        second_grad.reshape(3, 3, G, M), late[6], late[7], ew_grad, mine[0], mine[1], down_grad, va[0, 4], up_grad, mine[2],
        jnp.sum(va[0, 3] + va[1, 3]).reshape(1),
    )


def solution(mesh):
    rows = P("dp", None, None, "chan")
    placed = (
        rows, P("dp"), P("chan", None), P(), P(), P(), P(), P(), P(), P(), P(), P("chan", None), P("chan"), P("chan"),
        P("chan", None), P(), P(None, "chan"), P("chan"), P(), rows,
    )
    results = (
        rows, rows, P("chan", None), P(), P(), P(), P(), P(), P(), P(), P(), P("chan", None), P("chan"), P("chan"),
        P("chan", None), P(), P(None, "chan"), P("chan"), P(),
    )
    return jax.shard_map(body, mesh=mesh, in_specs=placed, out_specs=results, check_vma=False)
```
